256 devices in a mesh: chain: 16 (over x, y), gx: 2 (over z_lo), gy: 8 (over z_hi, core).
Axes of the slice: x: 4, y: 4, z: 8 (z_hi: 4, z_lo: 2; z = z_hi * 2 + z_lo), core: 2. Of those that a mesh axis runs over, the one named last changes fastest.
Arguments:
- initial_path: float32 [32, 64, 192, 256], P('chain', 'gx', 'gy'), may hold values from -3 to 3, as said below
Outputs:
- relaxed_path: float32 [32, 64, 192, 256], P('chain', 'gx', 'gy')
The draws below stay inside these ranges and needn't reach their ends.
Inputs may be any that keep to these rules, and one draw needn't show every extreme that they name: `initial_path`: each image lies near a point of a path between the two end states, with image-to-image noise.
All inputs are finite; a program needn't handle non-finite values.
Results may differ from the reference program's by a relative error of at most 0.00013.
Values sent between devices are 32-bit elements; how exact they have to be, the bound alone decides.
A program may use at most 64 MiB of HBM per device.

```python
import jax
import jax.numpy as jnp
from jax import lax

NZ = 256
RELAX = 3
OUTER = 1
IMAGES = 32
NX = 64
NY = 192


def draw_initial_path(key, part):
    ends_key = jax.random.fold_in(key, 11)
    gaps_key = jax.random.fold_in(key, 12)
    noise_key = jax.random.fold_in(key, 13)
    ends = -0.3 + 0.5 * jax.random.truncated_normal(ends_key, -4.0, 4.0, (2, NX, NY, NZ), jnp.float32)
    noise = 0.15 * jax.random.truncated_normal(noise_key, -4.0, 4.0, (IMAGES, NX, NY, NZ), jnp.float32)
    gaps = jax.random.uniform(gaps_key, (IMAGES - 1,), jnp.float32, 0.3, 1.7)
    position = jnp.concatenate([jnp.zeros((1,), jnp.float32), jnp.cumsum(gaps)]) / jnp.sum(gaps)
    weight = (4.0 * position * (1.0 - position))[:, None, None, None]
    shaped = position[:, None, None, None]
    return (1.0 - shaped) * ends[0][None] + shaped * ends[1][None] + weight * noise


def setup_inputs(seed: int = 0) -> dict:
    seeds = jax.random.split(jax.random.key(seed), 2)
    return {
        "initial_path": draw_initial_path(jax.random.fold_in(seeds[1], 71), 0),
    }


spacing = 0.7853981633974483
undercool = -0.25
time_step = 0.00025
step_size = 0.002
stiffness = 0.5
epsilon = 1e-06

def laplace(values):
    total = jnp.roll(values, -1, 0) + jnp.roll(values, 1, 0) + jnp.roll(values, -1, 1) + jnp.roll(values, 1, 1)
    total = total + jnp.roll(values, -1, 2) + jnp.roll(values, 1, 2)
    return (total - 6.0 * values) / (spacing * spacing)

def potential(field):
    first_lap = laplace(field)
    second_lap = laplace(first_lap)
    return (1.0 + undercool) * field + 2.0 * first_lap + second_lap + field * field * field

def relax_image(image):
    for relax_turn in range(RELAX):
        image = image + time_step * laplace(potential(image))
    return image

def reference(initial_path):
    field = initial_path
    cells = NX * NY * NZ
    for outer_turn in range(OUTER):
        field = lax.map(relax_image, field)
        chemical = lax.map(potential, field[1:-1])
        before = field[:-2]
        middle = field[1:-1]
        after = field[2:]
        tangent = after - before
        forward = after - middle
        backward = middle - before
        tangent_sq = lax.optimization_barrier(jnp.sum(tangent * tangent, axis=(1, 2, 3))) / cells
        forward_sq = lax.optimization_barrier(jnp.sum(forward * forward, axis=(1, 2, 3))) / cells
        backward_sq = lax.optimization_barrier(jnp.sum(backward * backward, axis=(1, 2, 3))) / cells
        intersection = lax.optimization_barrier(jnp.sum(chemical * tangent, axis=(1, 2, 3))) / cells
        scale = 1.0 / jnp.sqrt(tangent_sq + epsilon)
        unit = tangent * scale[:, None, None, None]
        along = intersection * scale
        spring = stiffness * (jnp.sqrt(forward_sq + epsilon) - jnp.sqrt(backward_sq + epsilon))
        moved = middle + step_size * (along[:, None, None, None] * unit - chemical) + spring[:, None, None, None] * unit
        field = jnp.concatenate([field[:1], moved, field[-1:]], axis=0)
    return field
```

```python
import jax
import jax.numpy as jnp
from jax import lax
from jax.experimental import pallas as pl
from jax.experimental.pallas import tpu as pltpu
from jax.sharding import PartitionSpec as P

RELAX = 3
spacing = 0.7853981633974483
undercool = -0.25
time_step = 0.00025
step_size = 0.002
stiffness = 0.5
epsilon = 1e-06

MESH = pl.DeviceIdType.MESH
LANES = 128
ROW = 8
XO = 3
YO = 8
H2 = spacing * spacing
H4 = H2 * H2
H6 = H4 * H2


def around(ref, i, x, y, first, last):
    a = ref[0, i, x, pl.ds(y, ROW), :]
    b = ref[1, i, x, pl.ds(y, ROW), :]
    ra, rb = pltpu.roll(a, 1, 1), pltpu.roll(b, 1, 1)
    qa, qb = pltpu.roll(a, LANES - 1, 1), pltpu.roll(b, LANES - 1, 1)
    za = jnp.where(first, rb, ra) + jnp.where(last, qb, qa)
    zb = jnp.where(first, ra, rb) + jnp.where(last, qa, qb)
    out = []
    for h, c, z in ((0, a, za), (1, b, zb)):
        s = ref[h, i, x, pl.ds(y - 1, ROW), :] + ref[h, i, x, pl.ds(y + 1, ROW), :]
        s = s + (ref[h, i, x - 1, pl.ds(y, ROW), :] + ref[h, i, x + 1, pl.ds(y, ROW), :])
        out.append((h, c, s + z))
    return out


def kernel(nx, ny, chain_n, gy_n, cells, in_ref, out_ref,
           f0, f1, f2, f3, w0, w1, w2, w3, g0, g1, g2, chem, nb, mine, rbuf,
           load_sem, halo_send, halo_recv, chain_send, chain_recv, red_send, red_recv, out_sem):
    fields, ws, gs = (f0, f1, f2, f3), (w0, w1, w2, w3), (g0, g1, g2)
    gx = lax.axis_index("gx")
    gy = lax.axis_index("gy")
    chain = lax.axis_index("chain")
    mate = 1 - gx
    up, down = lax.rem(gy + 1, gy_n), lax.rem(gy + gy_n - 1, gy_n)
    nxt, prv = lax.rem(chain + 1, chain_n), lax.rem(chain + chain_n - 1, chain_n)

    barrier = pltpu.get_barrier_semaphore()
    partners = (
        {"gx": mate}, {"gy": up}, {"gy": down}, {"gx": mate, "gy": up}, {"gx": mate, "gy": down},
        {"chain": nxt}, {"chain": prv},
    )
    for d in partners:
        pl.semaphore_signal(barrier, inc=1, device_id=d, device_id_type=MESH)

    cut = [nx // 2 + 3 * (RELAX - s) for s in range(RELAX + 1)]

    def layer(x):
        return gx * (nx - 1) + (1 - 2 * gx) * x

    def start_load(lo, hi, sem):
        def body(x, _):
            for h in range(2):
                pltpu.make_async_copy(
                    in_ref.at[:, layer(x), :, pl.ds(h * LANES, LANES)],
                    f0.at[h, :, XO + x, pl.ds(YO, ny), :], sem).start()
            return 0
        lax.fori_loop(lo, hi, body, 0)

    def wait_load(lo, hi, sem):
        view = f0.at[:, :, pl.ds(XO + lo, hi - lo), pl.ds(YO, ny), :]
        pltpu.make_async_copy(view, view, sem).wait()

    start_load(0, cut[0], load_sem.at[0])
    start_load(cut[0], nx, load_sem.at[1])

    def halo_copies(s, piece):
        f = fields[s]
        width = 3 if s < RELAX else 2
        lo, hi = (0, cut[s]) if piece == 0 else (cut[s], nx)
        rows = pl.ds(XO + lo, hi - lo)
        plan = [
            (f.at[:, :, rows, pl.ds(YO + ny - width, width), :],
             f.at[:, :, rows, pl.ds(YO - width, width), :], {"gy": up}),
            (f.at[:, :, rows, pl.ds(YO, width), :],
             f.at[:, :, rows, pl.ds(YO + ny, width), :], {"gy": down}),
        ]
        near = (lambda j: XO + j) if piece == 0 else (lambda j: XO + nx - 1 - j)
        far = (lambda j: XO - 1 - j) if piece == 0 else (lambda j: XO + nx + j)
        for j in range(width):
            plan.append((f.at[:, :, near(j), pl.ds(YO, ny), :],
                         f.at[:, :, far(j), pl.ds(YO, ny), :], {"gx": mate}))
        for j in range(width - 1):
            k = width - 1
            plan.append((f.at[:, :, near(j), pl.ds(YO + ny - k, k), :],
                         f.at[:, :, far(j), pl.ds(YO - k, k), :], {"gx": mate, "gy": up}))
            plan.append((f.at[:, :, near(j), pl.ds(YO, k), :],
                         f.at[:, :, far(j), pl.ds(YO + ny, k), :], {"gx": mate, "gy": down}))
        base = (2 * s + piece) * 9
        return [
            pltpu.make_async_remote_copy(
                src_ref=src, dst_ref=dst, send_sem=halo_send.at[base + n],
                recv_sem=halo_recv.at[base + n], device_id=d, device_id_type=MESH)
            for n, (src, dst, d) in enumerate(plan)
        ]

    halos = {(s, p): halo_copies(s, p) for s in range(RELAX + 1) for p in range(2)}

    def send_halo(s, p):
        for c in halos[s, p]:
            c.start()

    def wait_halo(s, p):
        for c in halos[s, p]:
            c.wait_recv()

    def chain_copies(p):
        lo, hi = (0, cut[RELAX]) if p == 0 else (cut[RELAX], nx)
        out = []
        for i, d in ((0, prv), (1, nxt)):
            out.append(pltpu.make_async_remote_copy(
                src_ref=f3.at[:, i, pl.ds(XO + lo, hi - lo), pl.ds(YO, ny), :],
                dst_ref=nb.at[:, 1 - i, pl.ds(lo, hi - lo), :, :],
                send_sem=chain_send.at[2 * p + i], recv_sem=chain_recv.at[2 * p + i],
                device_id={"chain": d}, device_id_type=MESH))
        return out

    chains = [chain_copies(p) for p in range(2)]

    lane = lax.broadcasted_iota(jnp.int32, (ROW, LANES), 1)
    first, last = lane == 0, lane == LANES - 1

    def span(p, start, mid, end):
        return (start, mid) if p == 0 else (mid, end)

    def pass_w(s, lo, hi):
        f, w = fields[s], ws[s]

        def body(x, _):
            for i in range(2):
                for y in range(YO - 2, YO + ny + 2, ROW):
                    for h, c, total in around(f, i, x, y, first, last):
                        w[h, i, x, pl.ds(y, ROW), :] = total + (2.0 * H2 - 6.0) * c
            return 0
        lax.fori_loop(XO + lo, XO + hi, body, 0)

    def bulk(f, h, i, x, y):
        c = f[h, i, x, pl.ds(y, ROW), :]
        return (c * c * H4 + (1.0 + undercool) * H4) * c

    def pass_g(s, lo, hi):
        f, w, g = fields[s], ws[s], gs[s]

        def body(x, _):
            for i in range(2):
                for y in range(YO - 1, YO + ny + 1, ROW):
                    for h, c, total in around(w, i, x, y, first, last):
                        g[h, i, x, pl.ds(y, ROW), :] = (total - 6.0 * c) + bulk(f, h, i, x, y)
            return 0
        lax.fori_loop(XO + lo, XO + hi, body, 0)

    def pass_f(s, lo, hi):
        f, g, new = fields[s], gs[s], fields[s + 1]

        def body(x, _):
            for i in range(2):
                for y in range(YO, YO + ny, ROW):
                    for h, c, total in around(g, i, x, y, first, last):
                        old = f[h, i, x, pl.ds(y, ROW), :]
                        new[h, i, x, pl.ds(y, ROW), :] = old + (time_step / H6) * (total - 6.0 * c)
            return 0
        lax.fori_loop(XO + lo, XO + hi, body, 0)

    def pass_chem(lo, hi):
        def body(x, _):
            for i in range(2):
                for y in range(YO, YO + ny, ROW):
                    for h, c, total in around(w3, i, x, y, first, last):
                        chem[h, i, x - XO, pl.ds(y - YO, ROW), :] = (
                            (total - 6.0 * c) + bulk(f3, h, i, x, y)) * (1.0 / H4)
            return 0
        lax.fori_loop(XO + lo, XO + hi, body, 0)

    def relax(s, p):
        c = cut[s]
        pass_w(s, *span(p, -2, c - 1, nx + 2))
        pass_g(s, *span(p, -1, c - 2, nx + 1))
        pass_f(s, *span(p, 0, c - 3, nx))

    def potential(p):
        c = cut[RELAX]
        pass_w(RELAX, *span(p, -1, c - 1, nx + 1))
        pass_chem(*span(p, 0, c - 2, nx))

    def sums(lo, hi, acc):
        def body(x, acc):
            acc = list(acc)
            for y in range(0, ny, ROW):
                for h in range(2):
                    a = f3[h, 0, XO + x, pl.ds(YO + y, ROW), :]
                    b = f3[h, 1, XO + x, pl.ds(YO + y, ROW), :]
                    before = nb[h, 0, x, pl.ds(y, ROW), :]
                    after = nb[h, 1, x, pl.ds(y, ROW), :]
                    ca = chem[h, 0, x, pl.ds(y, ROW), :]
                    cb = chem[h, 1, x, pl.ds(y, ROW), :]
                    ta, tb = b - before, after - a
                    d, low, high = b - a, a - before, after - b
                    terms = (ta * ta, tb * tb, low * low, d * d, high * high, ca * ta, cb * tb)
                    acc = [u + v for u, v in zip(acc, terms)]
            return tuple(acc)
        return lax.fori_loop(lo, hi, body, acc)

    pl.semaphore_wait(barrier, len(partners))
    wait_load(0, cut[0], load_sem.at[0])
    send_halo(0, 0)
    wait_load(cut[0], nx, load_sem.at[1])
    send_halo(0, 1)
    for s in range(RELAX):
        for p in range(2):
            wait_halo(s, p)
            relax(s, p)
            if s + 1 == RELAX:
                for c in chains[p]:
                    c.start()
            send_halo(s + 1, p)
    for p in range(2):
        wait_halo(RELAX, p)
        potential(p)
    acc = tuple(jnp.zeros((ROW, LANES), jnp.float32) for _ in range(7))
    mid = cut[RELAX] - 2
    for c in chains[0]:
        c.wait_recv()
    acc = sums(0, mid, acc)
    for c in chains[1]:
        c.wait_recv()
    acc = sums(mid, nx, acc)

    for n in range(7):
        mine[n : n + 1, :] = jnp.sum(acc[n], axis=0, keepdims=True)
    mine[7:8, :] = jnp.zeros((1, LANES), jnp.float32)
    group = 2 * gy_n
    me = gx * gy_n + gy
    copies = []
    for k in range(1, group):
        to = lax.rem(me + k, group)
        c = pltpu.make_async_remote_copy(
            src_ref=mine, dst_ref=rbuf.at[me], send_sem=red_send.at[k], recv_sem=red_recv.at[k],
            device_id={"gx": to // gy_n, "gy": lax.rem(to, gy_n)}, device_id_type=MESH)
        c.start()
        copies.append(c)
    rbuf[me] = mine[...]
    for c in copies:
        c.wait_recv()
    total = rbuf[0]
    for k in range(1, group):
        total = total + rbuf[k]

    def mean(n):
        return jnp.sum(total[n : n + 1, :], axis=1, keepdims=True) * (1.0 / cells)

    means = [mean(n) for n in range(7)]

    def factors(tangent_sq, forward_sq, backward_sq, intersection, keep):
        scale = 1.0 / jnp.sqrt(tangent_sq + epsilon)
        along = intersection * scale
        spring = stiffness * (jnp.sqrt(forward_sq + epsilon) - jnp.sqrt(backward_sq + epsilon))
        pull = (step_size * along + spring) * scale
        pull = jnp.where(keep, 0.0, pull)
        drop = jnp.where(keep, 0.0, jnp.full_like(pull, step_size))
        return jnp.broadcast_to(pull, (ROW, LANES)), jnp.broadcast_to(drop, (ROW, LANES))

    pull_a, drop_a = factors(means[0], means[3], means[2], means[5], chain == 0)
    pull_b, drop_b = factors(means[1], means[4], means[3], means[6], chain == chain_n - 1)

    def finish(x, _):
        for h in range(2):
            for y in range(0, ny, ROW):
                a = f3[h, 0, XO + x, pl.ds(YO + y, ROW), :]
                b = f3[h, 1, XO + x, pl.ds(YO + y, ROW), :]
                before = nb[h, 0, x, pl.ds(y, ROW), :]
                after = nb[h, 1, x, pl.ds(y, ROW), :]
                ca = chem[h, 0, x, pl.ds(y, ROW), :]
                cb = chem[h, 1, x, pl.ds(y, ROW), :]
                chem[h, 0, x, pl.ds(y, ROW), :] = a + (pull_a * (b - before) - drop_a * ca)
                chem[h, 1, x, pl.ds(y, ROW), :] = b + (pull_b * (after - a) - drop_b * cb)
            pltpu.make_async_copy(
                chem.at[h, :, x, :, :],
                out_ref.at[:, layer(x), :, pl.ds(h * LANES, LANES)], out_sem.at[0]).start()
        return 0

    lax.fori_loop(0, nx, finish, 0)
    pltpu.make_async_copy(chem, chem, out_sem.at[0]).wait()
    for c in [c for hs in halos.values() for c in hs] + chains[0] + chains[1] + copies:
        c.wait_send()


def per_device(chain_n, gx_n, gy_n, v):
    _, nx, ny, nz = v.shape
    cells = nx * gx_n * ny * gy_n * nz

    def body(*refs):
        kernel(nx, ny, chain_n, gy_n, cells, *refs)

    padded = pltpu.VMEM((2, 2, nx + 2 * XO, ny + 2 * YO, LANES), jnp.float32)
    plain = pltpu.VMEM((2, 2, nx, ny, LANES), jnp.float32)
    dma = pltpu.SemaphoreType.DMA
    return pl.pallas_call(
        body,
        out_shape=jax.ShapeDtypeStruct(v.shape, v.dtype),
        in_specs=[pl.BlockSpec(memory_space=pl.ANY)],
        out_specs=pl.BlockSpec(memory_space=pl.ANY),
        scratch_shapes=[padded] * 11 + [
            plain, plain,
            pltpu.VMEM((ROW, LANES), jnp.float32),
            pltpu.VMEM((2 * gy_n, ROW, LANES), jnp.float32),
            dma((2,)), dma((72,)), dma((72,)), dma((4,)), dma((4,)), dma((16,)), dma((16,)), dma((1,)),
        ],
        compiler_params=pltpu.CompilerParams(
            collective_id=0, has_side_effects=True, vmem_limit_bytes=60 * 1024 * 1024),
    )(v)


def solution(mesh):
    sizes = [mesh.shape[a] for a in ("chain", "gx", "gy")]
    spec = P("chain", "gx", "gy", None)
    return jax.shard_map(
        lambda v: per_device(*sizes, v), mesh=mesh, in_specs=(spec,), out_specs=spec, check_vma=False)
```

```python
import jax
import jax.numpy as jnp
from jax import lax
from jax.experimental import pallas as pl
from jax.experimental.pallas import tpu as pltpu
from jax.sharding import PartitionSpec as P

RELAX = 3
spacing = 0.7853981633974483
undercool = -0.25
time_step = 0.00025
step_size = 0.002
stiffness = 0.5
epsilon = 1e-06

MESH = pl.DeviceIdType.MESH
LANES = 128
ROW = 8
XO = 3
YO = 8
H2 = spacing * spacing
H4 = H2 * H2
H6 = H4 * H2
GROUP = 4


def around(ref, i, x, y):
    a = ref[0, i, x, pl.ds(y, ROW), :]
    b = ref[1, i, x, pl.ds(y, ROW), :]
    za = b + pltpu.roll(b, 1, 1)
    zb = a + pltpu.roll(a, LANES - 1, 1)
    out = []
    for h, c, z in ((0, a, za), (1, b, zb)):
        s = ref[h, i, x, pl.ds(y - 1, ROW), :] + ref[h, i, x, pl.ds(y + 1, ROW), :]
        s = s + (ref[h, i, x - 1, pl.ds(y, ROW), :] + ref[h, i, x + 1, pl.ds(y, ROW), :])
        out.append((h, c, s + z))
    return out


def rows_of(lo, hi, group, row):
    steps = (hi - lo) // group

    def body(n, _):
        for r in range(group):
            row(lo + n * group + r)
        return 0

    if steps:
        lax.fori_loop(0, steps, body, 0)
    for x in range(lo + steps * group, hi):
        row(x)


def kernel(nx, ny, chain_n, gy_n, cells, in_ref, out_ref,
           f0, f1, f2, f3, w0, w1, w2, w3, g0, g1, g2, chem, tang, nb, mine, rbuf,
           load_sem, halo_send, halo_recv, chain_send, chain_recv, red_send, red_recv, out_sem):
    fields, ws, gs = (f0, f1, f2, f3), (w0, w1, w2, w3), (g0, g1, g2)
    gx = lax.axis_index("gx")
    gy = lax.axis_index("gy")
    chain = lax.axis_index("chain")
    mate = 1 - gx
    up, down = lax.rem(gy + 1, gy_n), lax.rem(gy + gy_n - 1, gy_n)
    nxt, prv = lax.rem(chain + 1, chain_n), lax.rem(chain + chain_n - 1, chain_n)

    barrier = pltpu.get_barrier_semaphore()
    partners = (
        {"gx": mate}, {"gy": up}, {"gy": down}, {"gx": mate, "gy": up}, {"gx": mate, "gy": down},
        {"chain": nxt}, {"chain": prv},
    )
    for d in partners:
        pl.semaphore_signal(barrier, inc=1, device_id=d, device_id_type=MESH)

    cut = [nx // 2 + 3 * (RELAX - s) for s in range(RELAX + 1)]

    def layer(x):
        return gx * (nx - 1) + (1 - 2 * gx) * x

    def start_load(lo, hi, sem):
        def body(x, _):
            for h in range(2):
                pltpu.make_async_copy(
                    in_ref.at[:, layer(x), :, pl.ds(h * LANES, LANES)],
                    chem.at[h, :, x, :, :], sem).start()
            return 0
        lax.fori_loop(lo, hi, body, 0)

    def wait_load(lo, hi, sem):
        view = chem.at[:, :, pl.ds(lo, hi - lo), :, :]
        pltpu.make_async_copy(view, view, sem).wait()

    lane = lax.broadcasted_iota(jnp.int32, (ROW, LANES), 1)
    half = LANES // 2
    low_half, even = lane < half, lane % 2 == 0
    twice = (2 * lane) % LANES
    halved = lane // 2

    def pick(v, index):
        return jnp.take_along_axis(v, index, axis=1)

    def split(lo, hi):
        def row(x):
            for i in range(2):
                for y in range(0, ny, ROW):
                    a = chem[0, i, x, pl.ds(y, ROW), :] * H2
                    b = chem[1, i, x, pl.ds(y, ROW), :] * H2
                    f0[0, i, XO + x, pl.ds(YO + y, ROW), :] = jnp.where(
                        low_half, pick(a, twice), pick(b, twice))
                    f0[1, i, XO + x, pl.ds(YO + y, ROW), :] = jnp.where(
                        low_half, pick(a, twice + 1), pick(b, twice + 1))
        rows_of(lo, hi, 2, row)

    def joined(a, b):
        return (jnp.where(even, pick(a, halved), pick(b, halved)),
                jnp.where(even, pick(a, halved + half), pick(b, halved + half)))

    start_load(0, cut[0], load_sem.at[0])
    start_load(cut[0], nx, load_sem.at[1])

    def halo_copies(s, piece):
        f = fields[s]
        width = 3 if s < RELAX else 2
        lo, hi = (0, cut[s]) if piece == 0 else (cut[s], nx)
        rows = pl.ds(XO + lo, hi - lo)
        plan = [
            (f.at[:, :, rows, pl.ds(YO + ny - width, width), :],
             f.at[:, :, rows, pl.ds(YO - width, width), :], {"gy": up}),
            (f.at[:, :, rows, pl.ds(YO, width), :],
             f.at[:, :, rows, pl.ds(YO + ny, width), :], {"gy": down}),
        ]
        near = (lambda j: XO + j) if piece == 0 else (lambda j: XO + nx - 1 - j)
        far = (lambda j: XO - 1 - j) if piece == 0 else (lambda j: XO + nx + j)
        for j in range(width):
            plan.append((f.at[:, :, near(j), pl.ds(YO, ny), :],
                         f.at[:, :, far(j), pl.ds(YO, ny), :], {"gx": mate}))
        for j in range(width - 1):
            k = width - 1
            plan.append((f.at[:, :, near(j), pl.ds(YO + ny - k, k), :],
                         f.at[:, :, far(j), pl.ds(YO - k, k), :], {"gx": mate, "gy": up}))
            plan.append((f.at[:, :, near(j), pl.ds(YO, k), :],
                         f.at[:, :, far(j), pl.ds(YO + ny, k), :], {"gx": mate, "gy": down}))
        base = (2 * s + piece) * 9
        return [
            pltpu.make_async_remote_copy(
                src_ref=src, dst_ref=dst, send_sem=halo_send.at[base + n],
                recv_sem=halo_recv.at[base + n], device_id=d, device_id_type=MESH)
            for n, (src, dst, d) in enumerate(plan)
        ]

    halos = {(s, p): halo_copies(s, p) for s in range(RELAX + 1) for p in range(2)}

    def send_halo(s, p):
        for c in halos[s, p]:
            c.start()

    def wait_halo(s, p):
        for c in halos[s, p]:
            c.wait_recv()

    def chain_copies(p):
        lo, hi = (0, cut[RELAX]) if p == 0 else (cut[RELAX], nx)
        out = []
        for i, d in ((0, prv), (1, nxt)):
            out.append(pltpu.make_async_remote_copy(
                src_ref=f3.at[:, i, pl.ds(XO + lo, hi - lo), pl.ds(YO, ny), :],
                dst_ref=nb.at[:, 1 - i, pl.ds(lo, hi - lo), :, :],
                send_sem=chain_send.at[2 * p + i], recv_sem=chain_recv.at[2 * p + i],
                device_id={"chain": d}, device_id_type=MESH))
        return out

    chains = [chain_copies(p) for p in range(2)]

    def span(p, start, mid, end):
        return (start, mid) if p == 0 else (mid, end)

    def pass_w(s, lo, hi):
        f, w = fields[s], ws[s]

        def row(x):
            for i in range(2):
                for y in range(YO - 2, YO + ny + 2, ROW):
                    for h, c, total in around(f, i, x, y):
                        w[h, i, x, pl.ds(y, ROW), :] = total + (2.0 * H2 - 6.0) * c
        rows_of(XO + lo, XO + hi, GROUP, row)

    def bulk(f, h, i, x, y):
        c = f[h, i, x, pl.ds(y, ROW), :]
        return (c * c + (1.0 + undercool) * H4) * c

    def pass_g(s, lo, hi):
        f, w, g = fields[s], ws[s], gs[s]

        def row(x):
            for i in range(2):
                for y in range(YO - 1, YO + ny + 1, ROW):
                    for h, c, total in around(w, i, x, y):
                        g[h, i, x, pl.ds(y, ROW), :] = (total - 6.0 * c) + bulk(f, h, i, x, y)
        rows_of(XO + lo, XO + hi, GROUP, row)

    def pass_f(s, lo, hi):
        f, g, new = fields[s], gs[s], fields[s + 1]

        def row(x):
            for i in range(2):
                for y in range(YO, YO + ny, ROW):
                    for h, c, total in around(g, i, x, y):
                        old = f[h, i, x, pl.ds(y, ROW), :]
                        new[h, i, x, pl.ds(y, ROW), :] = old + (time_step / H6) * (total - 6.0 * c)
        rows_of(XO + lo, XO + hi, GROUP, row)

    def pass_chem(lo, hi):
        def row(x):
            for i in range(2):
                for y in range(YO, YO + ny, ROW):
                    for h, c, total in around(w3, i, x, y):
                        chem[h, i, x - XO, pl.ds(y - YO, ROW), :] = (
                            (total - 6.0 * c) + bulk(f3, h, i, x, y))
        rows_of(XO + lo, XO + hi, GROUP, row)

    def relax(s, p):
        c = cut[s]
        pass_w(s, *span(p, -2, c - 1, nx + 2))
        pass_g(s, *span(p, -1, c - 2, nx + 1))
        pass_f(s, *span(p, 0, c - 3, nx))

    def potential(p):
        c = cut[RELAX]
        pass_w(RELAX, *span(p, -1, c - 1, nx + 1))
        pass_chem(*span(p, 0, c - 2, nx))

    def sums(lo, hi, acc):
        def body(x, acc):
            acc = list(acc)
            for y in range(0, ny, ROW):
                for h in range(2):
                    a = f3[h, 0, XO + x, pl.ds(YO + y, ROW), :]
                    b = f3[h, 1, XO + x, pl.ds(YO + y, ROW), :]
                    before = nb[h, 0, x, pl.ds(y, ROW), :]
                    after = nb[h, 1, x, pl.ds(y, ROW), :]
                    ca = chem[h, 0, x, pl.ds(y, ROW), :]
                    cb = chem[h, 1, x, pl.ds(y, ROW), :]
                    ta, tb = b - before, after - a
                    d, low, high = b - a, a - before, after - b
                    terms = (ta * ta, tb * tb, low * low, d * d, high * high, ca * ta, cb * tb)
                    acc = [u + v for u, v in zip(acc, terms)]
            return tuple(acc)
        return lax.fori_loop(lo, hi, body, acc)

    wait_load(0, cut[0], load_sem.at[0])
    split(0, cut[0])
    wait_load(cut[0], nx, load_sem.at[1])
    split(cut[0], nx)
    pl.semaphore_wait(barrier, len(partners))
    send_halo(0, 0)
    send_halo(0, 1)
    for s in range(RELAX):
        for p in range(2):
            wait_halo(s, p)
            relax(s, p)
            if s + 1 == RELAX:
                for c in chains[p]:
                    c.start()
            send_halo(s + 1, p)
    for p in range(2):
        wait_halo(RELAX, p)
        potential(p)
    acc = tuple(jnp.zeros((ROW, LANES), jnp.float32) for _ in range(7))
    mid = cut[RELAX] - 2
    for c in chains[0]:
        c.wait_recv()
    acc = sums(0, mid, acc)
    for c in chains[1]:
        c.wait_recv()
    acc = sums(mid, nx, acc)

    for n in range(7):
        mine[n : n + 1, :] = jnp.sum(acc[n], axis=0, keepdims=True)
    mine[7:8, :] = jnp.zeros((1, LANES), jnp.float32)
    group = 2 * gy_n
    me = gx * gy_n + gy
    copies = []
    for k in range(1, group):
        to = lax.rem(me + k, group)
        c = pltpu.make_async_remote_copy(
            src_ref=mine, dst_ref=rbuf.at[me], send_sem=red_send.at[k], recv_sem=red_recv.at[k],
            device_id={"gx": to // gy_n, "gy": lax.rem(to, gy_n)}, device_id_type=MESH)
        c.start()
        copies.append(c)
    rbuf[me] = mine[...]

    drops = [jnp.where(chain == end, 0.0, step_size / H6) for end in (0, chain_n - 1)]

    def prepare(x):
        for y in range(0, ny, ROW):
            at = pl.ds(y, ROW)
            f = [[f3[h, i, XO + x, pl.ds(YO + y, ROW), :] for h in range(2)] for i in range(2)]
            for i in range(2):
                rest = joined(*[f[i][h] * (1.0 / H2) - drops[i] * chem[h, i, x, at, :] for h in range(2)])
                if i == 0:
                    t = joined(*[f[1][h] - nb[h, 0, x, at, :] for h in range(2)])
                else:
                    t = joined(*[nb[h, 1, x, at, :] - f[0][h] for h in range(2)])
                for h in range(2):
                    chem[h, i, x, at, :] = rest[h]
                    tang[h, i, x, at, :] = t[h]

    rows_of(0, nx, 2, prepare)
    for c in copies:
        c.wait_recv()
    total = rbuf[0]
    for k in range(1, group):
        total = total + rbuf[k]

    def mean(n, scaling):
        return jnp.sum(total[n : n + 1, :], axis=1, keepdims=True) * (1.0 / (cells * scaling))

    squares = [mean(n, H4) for n in range(5)]
    products = [mean(n, H6 * H2) for n in (5, 6)]

    def pull_of(tangent_sq, forward_sq, backward_sq, intersection, keep):
        scale = 1.0 / jnp.sqrt(tangent_sq + epsilon)
        along = intersection * scale
        spring = stiffness * (jnp.sqrt(forward_sq + epsilon) - jnp.sqrt(backward_sq + epsilon))
        pull = (step_size * along + spring) * scale * (1.0 / H2)
        return jnp.broadcast_to(jnp.where(keep, 0.0, pull), (ROW, LANES))

    pulls = (pull_of(squares[0], squares[3], squares[2], products[0], chain == 0),
             pull_of(squares[1], squares[4], squares[3], products[1], chain == chain_n - 1))

    def finish(x):
        for h in range(2):
            for y in range(0, ny, ROW):
                for i in range(2):
                    at = pl.ds(y, ROW)
                    tang[h, i, x, at, :] = chem[h, i, x, at, :] + pulls[i] * tang[h, i, x, at, :]
            pltpu.make_async_copy(
                tang.at[h, :, x, :, :],
                out_ref.at[:, layer(x), :, pl.ds(h * LANES, LANES)], out_sem.at[0]).start()

    rows_of(0, nx, 4, finish)
    pltpu.make_async_copy(tang, tang, out_sem.at[0]).wait()
    for c in [c for hs in halos.values() for c in hs] + chains[0] + chains[1] + copies:
        c.wait_send()


def per_device(chain_n, gx_n, gy_n, v):
    _, nx, ny, nz = v.shape
    cells = nx * gx_n * ny * gy_n * nz

    def body(*refs):
        kernel(nx, ny, chain_n, gy_n, cells, *refs)

    padded = pltpu.VMEM((2, 2, nx + 2 * XO, ny + 2 * YO, LANES), jnp.float32)
    plain = pltpu.VMEM((2, 2, nx, ny, LANES), jnp.float32)
    dma = pltpu.SemaphoreType.DMA
    return pl.pallas_call(
        body,
        out_shape=jax.ShapeDtypeStruct(v.shape, v.dtype),
        in_specs=[pl.BlockSpec(memory_space=pl.ANY)],
        out_specs=pl.BlockSpec(memory_space=pl.ANY),
        scratch_shapes=[padded] * 11 + [
            plain, plain, plain,
            pltpu.VMEM((ROW, LANES), jnp.float32),
            pltpu.VMEM((2 * gy_n, ROW, LANES), jnp.float32),
            dma((2,)), dma((72,)), dma((72,)), dma((4,)), dma((4,)), dma((16,)), dma((16,)), dma((1,)),
        ],
        compiler_params=pltpu.CompilerParams(
            collective_id=0, has_side_effects=True, vmem_limit_bytes=60 * 1024 * 1024),
    )(v)


def solution(mesh):
    sizes = [mesh.shape[a] for a in ("chain", "gx", "gy")]
    spec = P("chain", "gx", "gy", None)
    return jax.shard_map(
        lambda v: per_device(*sizes, v), mesh=mesh, in_specs=(spec,), out_specs=spec, check_vma=False)
```

```python
import jax
import jax.numpy as jnp
from jax import lax
from jax.experimental import pallas as pl
from jax.experimental.pallas import tpu as pltpu
from jax.sharding import PartitionSpec as P

RELAX = 3
spacing = 0.7853981633974483
undercool = -0.25
time_step = 0.00025
step_size = 0.002
stiffness = 0.5
epsilon = 1e-06

MESH = pl.DeviceIdType.MESH
LANES = 128
ROW = 8
XO = 3
YO = 8
H2 = spacing * spacing
H4 = H2 * H2
H6 = H4 * H2
GROUP = 8
MID = 21
ORDER = "sa0 sb0 sc0 ra0 sa1 rb0 sb1 sd0 ra1 sa2 rb1 sb2 rc0 sc1 ra2 xa rd0 sd1 rb2 xb rc1 sc2 sa3 rd1 sd2 sb3"
ORDER += " rc2 xc sc3 rd2 xd sd3 pa3 pb3 t0 pc3 pd3 t1"


def around(ref, i, x, y):
    a = ref[0, i, x, pl.ds(y, ROW), :]
    b = ref[1, i, x, pl.ds(y, ROW), :]
    za = b + pltpu.roll(b, 1, 1)
    zb = a + pltpu.roll(a, LANES - 1, 1)
    out = []
    for h, c, z in ((0, a, za), (1, b, zb)):
        s = ref[h, i, x, pl.ds(y - 1, ROW), :] + ref[h, i, x, pl.ds(y + 1, ROW), :]
        s = s + (ref[h, i, x - 1, pl.ds(y, ROW), :] + ref[h, i, x + 1, pl.ds(y, ROW), :])
        out.append((h, c, s + z))
    return out


def rows_of(lo, hi, group, row):
    steps = (hi - lo) // group

    def body(n, _):
        for r in range(group):
            row(lo + n * group + r)
        return 0

    if steps:
        lax.fori_loop(0, steps, body, 0)
    for x in range(lo + steps * group, hi):
        row(x)


def kernel(nx, ny, chain_n, gy_n, cells, in_ref, out_ref,
           f0, f1, f2, f3, w0, w1, w2, w3, g0, g1, g2, chem, tang, nb, mine, rbuf,
           load_sem, halo_send, halo_recv, chain_send, chain_recv, red_send, red_recv, out_sem):
    fields, ws, gs = (f0, f1, f2, f3), (w0, w1, w2, w3), (g0, g1, g2)
    gx = lax.axis_index("gx")
    gy = lax.axis_index("gy")
    chain = lax.axis_index("chain")
    mate = 1 - gx
    up, down = lax.rem(gy + 1, gy_n), lax.rem(gy + gy_n - 1, gy_n)
    nxt, prv = lax.rem(chain + 1, chain_n), lax.rem(chain + chain_n - 1, chain_n)

    barrier = pltpu.get_barrier_semaphore()
    partners = (
        {"gx": mate}, {"gy": up}, {"gy": down}, {"gx": mate, "gy": up}, {"gx": mate, "gy": down},
        {"chain": nxt}, {"chain": prv},
    )
    for d in partners:
        pl.semaphore_signal(barrier, inc=1, device_id=d, device_id_type=MESH)

    cut = [MID * nx // 32 + 3 * (RELAX - s) for s in range(RELAX + 1)]

    def layer(x):
        return gx * (nx - 1) + (1 - 2 * gx) * x

    def start_load(lo, hi, sem):
        def body(x, _):
            for h in range(2):
                pltpu.make_async_copy(
                    in_ref.at[:, layer(x), :, pl.ds(h * LANES, LANES)],
                    chem.at[h, :, x, :, :], sem).start()
            return 0
        lax.fori_loop(lo, hi, body, 0)

    def wait_load(lo, hi, sem):
        view = chem.at[:, :, pl.ds(lo, hi - lo), :, :]
        pltpu.make_async_copy(view, view, sem).wait()

    lane = lax.broadcasted_iota(jnp.int32, (ROW, LANES), 1)
    half = LANES // 2
    low_half, even = lane < half, lane % 2 == 0
    twice = (2 * lane) % LANES
    halved = lane // 2

    def pick(v, index):
        return jnp.take_along_axis(v, index, axis=1)

    def split(lo, hi):
        def row(x):
            for i in range(2):
                for y in range(0, ny, ROW):
                    a = chem[0, i, x, pl.ds(y, ROW), :] * H2
                    b = chem[1, i, x, pl.ds(y, ROW), :] * H2
                    f0[0, i, XO + x, pl.ds(YO + y, ROW), :] = jnp.where(
                        low_half, pick(a, twice), pick(b, twice))
                    f0[1, i, XO + x, pl.ds(YO + y, ROW), :] = jnp.where(
                        low_half, pick(a, twice + 1), pick(b, twice + 1))
        rows_of(lo, hi, 2, row)

    def joined(a, b):
        return (jnp.where(even, pick(a, halved), pick(b, halved)),
                jnp.where(even, pick(a, halved + half), pick(b, halved + half)))

    start_load(0, cut[0], load_sem.at[0])
    start_load(cut[0], nx, load_sem.at[1])

    def halo_copies(s, i, piece):
        f = fields[s]
        width = 3 if s < RELAX else 2
        lo, hi = span(piece, 0, cut[s], nx)
        rows = pl.ds(XO + lo, hi - lo)
        plan = [
            (f.at[:, i, rows, pl.ds(YO + ny - width, width), :],
             f.at[:, i, rows, pl.ds(YO - width, width), :], {"gy": up}),
            (f.at[:, i, rows, pl.ds(YO, width), :],
             f.at[:, i, rows, pl.ds(YO + ny, width), :], {"gy": down}),
        ]
        near = (lambda j: XO + j) if piece == 0 else (lambda j: XO + nx - 1 - j)
        far = (lambda j: XO - 1 - j) if piece == 0 else (lambda j: XO + nx + j)
        for j in range(width):
            plan.append((f.at[:, i, near(j), pl.ds(YO, ny), :],
                         f.at[:, i, far(j), pl.ds(YO, ny), :], {"gx": mate}))
        for j in range(width - 1):
            k = width - 1
            plan.append((f.at[:, i, near(j), pl.ds(YO + ny - k, k), :],
                         f.at[:, i, far(j), pl.ds(YO - k, k), :], {"gx": mate, "gy": up}))
            plan.append((f.at[:, i, near(j), pl.ds(YO, k), :],
                         f.at[:, i, far(j), pl.ds(YO + ny, k), :], {"gx": mate, "gy": down}))
        base = ((2 * s + piece) * 2 + i) * 9
        return [
            pltpu.make_async_remote_copy(
                src_ref=src, dst_ref=dst, send_sem=halo_send.at[base + n],
                recv_sem=halo_recv.at[base + n], device_id=d, device_id_type=MESH)
            for n, (src, dst, d) in enumerate(plan)
        ]

    def span(p, start, mid, end):
        return (start, mid) if p == 0 else (mid, end)

    halos = {(s, i, p): halo_copies(s, i, p)
             for s in range(RELAX + 1) for i in range(2) for p in range(2)}

    has = (chain > 0, chain < chain_n - 1)

    def chain_copy(i, p):
        lo, hi = span(p, 0, cut[RELAX], nx)
        return pltpu.make_async_remote_copy(
            src_ref=f3.at[:, i, pl.ds(XO + lo, hi - lo), pl.ds(YO, ny), :],
            dst_ref=nb.at[:, 1 - i, pl.ds(lo, hi - lo), :, :],
            send_sem=chain_send.at[2 * p + i], recv_sem=chain_recv.at[2 * p + i],
            device_id={"chain": (prv, nxt)[i]}, device_id_type=MESH)

    chains = {(i, p): chain_copy(i, p) for i in range(2) for p in range(2)}

    def pass_w(s, i, lo, hi):
        f, w = fields[s], ws[s]

        def row(x):
            for y in range(YO - 2, YO + ny + 2, ROW):
                for h, c, total in around(f, i, x, y):
                    w[h, i, x, pl.ds(y, ROW), :] = total + (2.0 * H2 - 6.0) * c
        rows_of(XO + lo, XO + hi, GROUP, row)

    def bulk(f, h, i, x, y):
        c = f[h, i, x, pl.ds(y, ROW), :]
        return (c * c + (1.0 + undercool) * H4) * c

    def pass_g(s, i, lo, hi):
        f, w, g = fields[s], ws[s], gs[s]

        def row(x):
            for y in range(YO - 1, YO + ny + 1, ROW):
                for h, c, total in around(w, i, x, y):
                    g[h, i, x, pl.ds(y, ROW), :] = (total - 6.0 * c) + bulk(f, h, i, x, y)
        rows_of(XO + lo, XO + hi, GROUP, row)

    def pass_f(s, i, lo, hi):
        f, g, new = fields[s], gs[s], fields[s + 1]

        def row(x):
            for y in range(YO, YO + ny, ROW):
                for h, c, total in around(g, i, x, y):
                    old = f[h, i, x, pl.ds(y, ROW), :]
                    new[h, i, x, pl.ds(y, ROW), :] = old + (time_step / H6) * (total - 6.0 * c)
        rows_of(XO + lo, XO + hi, GROUP, row)

    def pass_chem(i, lo, hi):
        def row(x):
            for y in range(YO, YO + ny, ROW):
                for h, c, total in around(w3, i, x, y):
                    chem[h, i, x - XO, pl.ds(y - YO, ROW), :] = (
                        (total - 6.0 * c) + bulk(f3, h, i, x, y))
        rows_of(XO + lo, XO + hi, GROUP, row)

    def relax(s, i, p):
        c = cut[s]
        pass_w(s, i, *span(p, -2, c - 1, nx + 2))
        pass_g(s, i, *span(p, -1, c - 2, nx + 1))
        pass_f(s, i, *span(p, 0, c - 3, nx))

    def potential(i, p):
        c = cut[RELAX]
        pass_w(RELAX, i, *span(p, -1, c - 1, nx + 1))
        pass_chem(i, *span(p, 0, c - 2, nx))

    def sums(lo, hi, acc):
        def body(x, acc):
            acc = list(acc)
            for y in range(0, ny, ROW):
                for h in range(2):
                    a = f3[h, 0, XO + x, pl.ds(YO + y, ROW), :]
                    b = f3[h, 1, XO + x, pl.ds(YO + y, ROW), :]
                    before = nb[h, 0, x, pl.ds(y, ROW), :]
                    after = nb[h, 1, x, pl.ds(y, ROW), :]
                    ca = chem[h, 0, x, pl.ds(y, ROW), :]
                    cb = chem[h, 1, x, pl.ds(y, ROW), :]
                    ta, tb = b - before, after - a
                    d, low, high = b - a, a - before, after - b
                    terms = (ta * ta, tb * tb, low * low, d * d, high * high, ca * ta, cb * tb)
                    acc = [u + v for u, v in zip(acc, terms)]
            return tuple(acc)
        return lax.fori_loop(lo, hi, body, acc)

    wait_load(0, cut[0], load_sem.at[0])
    split(0, cut[0])
    wait_load(cut[0], nx, load_sem.at[1])
    split(cut[0], nx)
    pl.semaphore_wait(barrier, len(partners))
    acc = tuple(jnp.zeros((ROW, LANES), jnp.float32) for _ in range(7))
    for word in ORDER.split():
        if word[0] == "t":
            p = int(word[1])
            for i in range(2):
                @pl.when(has[1 - i])
                def _():
                    chains[i, p].wait_recv()
            acc = sums(*span(p, 0, cut[RELAX] - 2, nx), acc)
            continue
        i, p = "abcd".index(word[1]) % 2, "abcd".index(word[1]) // 2
        if word[0] == "x":
            @pl.when(has[i])
            def _():
                chains[i, p].start()
            continue
        s = int(word[2])
        for c in halos[s, i, p]:
            if word[0] == "s":
                c.start()
            else:
                c.wait_recv()
        if word[0] == "r":
            relax(s, i, p)
        if word[0] == "p":
            potential(i, p)

    for n in range(7):
        mine[n : n + 1, :] = jnp.sum(acc[n], axis=0, keepdims=True)
    mine[7:8, :] = jnp.zeros((1, LANES), jnp.float32)
    group = 2 * gy_n
    me = gx * gy_n + gy
    copies = []
    for k in range(1, group):
        to = lax.rem(me + k, group)
        c = pltpu.make_async_remote_copy(
            src_ref=mine, dst_ref=rbuf.at[me], send_sem=red_send.at[k], recv_sem=red_recv.at[k],
            device_id={"gx": to // gy_n, "gy": lax.rem(to, gy_n)}, device_id_type=MESH)
        c.start()
        copies.append(c)
    rbuf[me] = mine[...]

    drops = [jnp.where(chain == end, 0.0, step_size / H6) for end in (0, chain_n - 1)]

    def prepare(x):
        for y in range(0, ny, ROW):
            at = pl.ds(y, ROW)
            f = [[f3[h, i, XO + x, pl.ds(YO + y, ROW), :] for h in range(2)] for i in range(2)]
            for i in range(2):
                rest = joined(*[f[i][h] * (1.0 / H2) - drops[i] * chem[h, i, x, at, :] for h in range(2)])
                if i == 0:
                    t = joined(*[jnp.where(has[0], f[1][h] - nb[h, 0, x, at, :], 0.0) for h in range(2)])
                else:
                    t = joined(*[jnp.where(has[1], nb[h, 1, x, at, :] - f[0][h], 0.0) for h in range(2)])
                for h in range(2):
                    chem[h, i, x, at, :] = rest[h]
                    tang[h, i, x, at, :] = t[h]

    rows_of(0, nx, 2, prepare)
    for c in copies:
        c.wait_recv()
    total = rbuf[0]
    for k in range(1, group):
        total = total + rbuf[k]

    def mean(n, scaling):
        return jnp.sum(total[n : n + 1, :], axis=1, keepdims=True) * (1.0 / (cells * scaling))

    squares = [mean(n, H4) for n in range(5)]
    products = [mean(n, H6 * H2) for n in (5, 6)]

    def pull_of(tangent_sq, forward_sq, backward_sq, intersection, keep):
        scale = 1.0 / jnp.sqrt(tangent_sq + epsilon)
        along = intersection * scale
        spring = stiffness * (jnp.sqrt(forward_sq + epsilon) - jnp.sqrt(backward_sq + epsilon))
        pull = (step_size * along + spring) * scale * (1.0 / H2)
        return jnp.broadcast_to(jnp.where(keep, 0.0, pull), (ROW, LANES))

    pulls = (pull_of(squares[0], squares[3], squares[2], products[0], chain == 0),
             pull_of(squares[1], squares[4], squares[3], products[1], chain == chain_n - 1))

    def finish(x):
        for h in range(2):
            for y in range(0, ny, ROW):
                for i in range(2):
                    at = pl.ds(y, ROW)
                    tang[h, i, x, at, :] = chem[h, i, x, at, :] + pulls[i] * tang[h, i, x, at, :]
            pltpu.make_async_copy(
                tang.at[h, :, x, :, :],
                out_ref.at[:, layer(x), :, pl.ds(h * LANES, LANES)], out_sem.at[0]).start()

    rows_of(0, nx, 4, finish)
    pltpu.make_async_copy(tang, tang, out_sem.at[0]).wait()
    for c in [c for hs in halos.values() for c in hs] + copies:
        c.wait_send()
    for i in range(2):
        @pl.when(has[i])
        def _():
            for p in range(2):
                chains[i, p].wait_send()


def per_device(chain_n, gx_n, gy_n, v):
    _, nx, ny, nz = v.shape
    cells = nx * gx_n * ny * gy_n * nz

    def body(*refs):
        kernel(nx, ny, chain_n, gy_n, cells, *refs)

    padded = pltpu.VMEM((2, 2, nx + 2 * XO, ny + 2 * YO, LANES), jnp.float32)
    plain = pltpu.VMEM((2, 2, nx, ny, LANES), jnp.float32)
    dma = pltpu.SemaphoreType.DMA
    return pl.pallas_call(
        body,
        out_shape=jax.ShapeDtypeStruct(v.shape, v.dtype),
        in_specs=[pl.BlockSpec(memory_space=pl.ANY)],
        out_specs=pl.BlockSpec(memory_space=pl.ANY),
        scratch_shapes=[padded] * 11 + [
            plain, plain, plain,
            pltpu.VMEM((ROW, LANES), jnp.float32),
            pltpu.VMEM((2 * gy_n, ROW, LANES), jnp.float32),
            dma((2,)), dma((144,)), dma((144,)), dma((4,)), dma((4,)), dma((16,)), dma((16,)), dma((1,)),
        ],
        compiler_params=pltpu.CompilerParams(
            collective_id=0, has_side_effects=True, vmem_limit_bytes=60 * 1024 * 1024),
    )(v)


def solution(mesh):
    sizes = [mesh.shape[a] for a in ("chain", "gx", "gy")]
    spec = P("chain", "gx", "gy", None)
    return jax.shard_map(
        lambda v: per_device(*sizes, v), mesh=mesh, in_specs=(spec,), out_specs=spec, check_vma=False)
```

```python
import jax
import jax.numpy as jnp
from jax import lax
from jax.experimental import pallas as pl
from jax.experimental.pallas import tpu as pltpu
from jax.sharding import PartitionSpec as P

RELAX = 3
spacing = 0.7853981633974483
undercool = -0.25
time_step = 0.00025
step_size = 0.002
stiffness = 0.5
epsilon = 1e-06

MESH = pl.DeviceIdType.MESH
LANES = 128
ROW = 8
XO = 3
YO = 8
H2 = spacing * spacing
H4 = H2 * H2
H6 = H4 * H2
GROUP = 8
MID = 21
ORDER = (
    "sa0", "sb0", "sc0", "ra0", "sa1", "rb0", "sb1", "sd0", "ra1", "sa2", "rb1", "sb2", "rc0",
    "sc1", "ra2", "xa", "rd0", "sd1", "rb2", "xb", "rc1", "sc2", "sa3", "rd1", "sd2", "sb3", "rc2",
    "xc", "sc3", "rd2", "xd", "sd3", "pa3", "pb3", "t0", "pc3", "pd3", "t1",
)


def around(ref, i, x, y):
    a = ref[0, i, x, pl.ds(y, ROW), :]
    b = ref[1, i, x, pl.ds(y, ROW), :]
    za = b + pltpu.roll(b, 1, 1)
    zb = a + pltpu.roll(a, LANES - 1, 1)
    out = []
    for h, c, z in ((0, a, za), (1, b, zb)):
        s = ref[h, i, x, pl.ds(y - 1, ROW), :] + ref[h, i, x, pl.ds(y + 1, ROW), :]
        s = s + (ref[h, i, x - 1, pl.ds(y, ROW), :] + ref[h, i, x + 1, pl.ds(y, ROW), :])
        out.append((h, c, s + z))
    return out


def rows_of(lo, hi, group, row):
    steps = (hi - lo) // group

    def body(n, _):
        for r in range(group):
            row(lo + n * group + r)
        return 0

    if steps:
        lax.fori_loop(0, steps, body, 0)
    for x in range(lo + steps * group, hi):
        row(x)


def kernel(nx, ny, chain_n, gy_n, cells, in_ref, rest_ref, tangent_ref, pull_ref,
           f0, f1, f2, f3, w0, w1, w2, w3, g0, g1, g2, chem, tang, nb, mine, rbuf,
           load_sem, halo_send, halo_recv, chain_send, chain_recv, red_send, red_recv, out_sem):
    fields, ws, gs = (f0, f1, f2, f3), (w0, w1, w2, w3), (g0, g1, g2)
    gx = lax.axis_index("gx")
    gy = lax.axis_index("gy")
    chain = lax.axis_index("chain")
    mate = 1 - gx
    up, down = lax.rem(gy + 1, gy_n), lax.rem(gy + gy_n - 1, gy_n)
    nxt, prv = lax.rem(chain + 1, chain_n), lax.rem(chain + chain_n - 1, chain_n)

    barrier = pltpu.get_barrier_semaphore()
    partners = (
        {"gx": mate}, {"gy": up}, {"gy": down}, {"gx": mate, "gy": up}, {"gx": mate, "gy": down},
        {"chain": nxt}, {"chain": prv},
    )
    for d in partners:
        pl.semaphore_signal(barrier, inc=1, device_id=d, device_id_type=MESH)

    cut = [MID * nx // 32 + 3 * (RELAX - s) for s in range(RELAX + 1)]

    def layer(x):
        return gx * (nx - 1) + (1 - 2 * gx) * x

    def start_load(lo, hi, sem):
        def body(x, _):
            for h in range(2):
                pltpu.make_async_copy(
                    in_ref.at[:, layer(x), :, pl.ds(h * LANES, LANES)],
                    chem.at[h, :, x, :, :], sem).start()
            return 0
        lax.fori_loop(lo, hi, body, 0)

    def wait_load(lo, hi, sem):
        view = chem.at[:, :, pl.ds(lo, hi - lo), :, :]
        pltpu.make_async_copy(view, view, sem).wait()

    lane = lax.broadcasted_iota(jnp.int32, (ROW, LANES), 1)
    half = LANES // 2
    low_half, even = lane < half, lane % 2 == 0
    twice = (2 * lane) % LANES
    halved = lane // 2

    def pick(v, index):
        return jnp.take_along_axis(v, index, axis=1)

    def split(lo, hi):
        def row(x):
            for i in range(2):
                for y in range(0, ny, ROW):
                    a = chem[0, i, x, pl.ds(y, ROW), :] * H2
                    b = chem[1, i, x, pl.ds(y, ROW), :] * H2
                    f0[0, i, XO + x, pl.ds(YO + y, ROW), :] = jnp.where(
                        low_half, pick(a, twice), pick(b, twice))
                    f0[1, i, XO + x, pl.ds(YO + y, ROW), :] = jnp.where(
                        low_half, pick(a, twice + 1), pick(b, twice + 1))
        rows_of(lo, hi, 2, row)

    def joined(a, b):
        return (jnp.where(even, pick(a, halved), pick(b, halved)),
                jnp.where(even, pick(a, halved + half), pick(b, halved + half)))

    start_load(0, cut[0], load_sem.at[0])
    start_load(cut[0], nx, load_sem.at[1])

    def halo_copies(s, i, piece):
        f = fields[s]
        width = 3 if s < RELAX else 2
        lo, hi = span(piece, 0, cut[s], nx)
        rows = pl.ds(XO + lo, hi - lo)
        plan = [
            (f.at[:, i, rows, pl.ds(YO + ny - width, width), :],
             f.at[:, i, rows, pl.ds(YO - width, width), :], {"gy": up}),
            (f.at[:, i, rows, pl.ds(YO, width), :],
             f.at[:, i, rows, pl.ds(YO + ny, width), :], {"gy": down}),
        ]
        near = (lambda j: XO + j) if piece == 0 else (lambda j: XO + nx - 1 - j)
        far = (lambda j: XO - 1 - j) if piece == 0 else (lambda j: XO + nx + j)
        for j in range(width):
            plan.append((f.at[:, i, near(j), pl.ds(YO, ny), :],
                         f.at[:, i, far(j), pl.ds(YO, ny), :], {"gx": mate}))
        for j in range(width - 1):
            k = width - 1
            plan.append((f.at[:, i, near(j), pl.ds(YO + ny - k, k), :],
                         f.at[:, i, far(j), pl.ds(YO - k, k), :], {"gx": mate, "gy": up}))
            plan.append((f.at[:, i, near(j), pl.ds(YO, k), :],
                         f.at[:, i, far(j), pl.ds(YO + ny, k), :], {"gx": mate, "gy": down}))
        plan.sort(key=lambda copy: -len(copy[2]))
        base = ((2 * s + piece) * 2 + i) * 9
        return [
            pltpu.make_async_remote_copy(
                src_ref=src, dst_ref=dst, send_sem=halo_send.at[base + n],
                recv_sem=halo_recv.at[base + n], device_id=d, device_id_type=MESH)
            for n, (src, dst, d) in enumerate(plan)
        ]

    def span(p, start, mid, end):
        return (start, mid) if p == 0 else (mid, end)

    halos = {(s, i, p): halo_copies(s, i, p)
             for s in range(RELAX + 1) for i in range(2) for p in range(2)}

    has = (chain > 0, chain < chain_n - 1)

    def chain_copy(i, p):
        lo, hi = span(p, 0, cut[RELAX], nx)
        return pltpu.make_async_remote_copy(
            src_ref=f3.at[:, i, pl.ds(XO + lo, hi - lo), pl.ds(YO, ny), :],
            dst_ref=nb.at[:, 1 - i, pl.ds(lo, hi - lo), :, :],
            send_sem=chain_send.at[2 * p + i], recv_sem=chain_recv.at[2 * p + i],
            device_id={"chain": (prv, nxt)[i]}, device_id_type=MESH)

    chains = {(i, p): chain_copy(i, p) for i in range(2) for p in range(2)}

    def pass_w(s, i, lo, hi):
        f, w = fields[s], ws[s]

        def row(x):
            for y in range(YO - 2, YO + ny + 2, ROW):
                for h, c, total in around(f, i, x, y):
                    w[h, i, x, pl.ds(y, ROW), :] = total + (2.0 * H2 - 6.0) * c
        rows_of(XO + lo, XO + hi, GROUP, row)

    def bulk(f, h, i, x, y):
        c = f[h, i, x, pl.ds(y, ROW), :]
        return (c * c + (1.0 + undercool) * H4) * c

    def pass_g(s, i, lo, hi):
        f, w, g = fields[s], ws[s], gs[s]

        def row(x):
            for y in range(YO - 1, YO + ny + 1, ROW):
                for h, c, total in around(w, i, x, y):
                    g[h, i, x, pl.ds(y, ROW), :] = (total - 6.0 * c) + bulk(f, h, i, x, y)
        rows_of(XO + lo, XO + hi, GROUP, row)

    def pass_f(s, i, lo, hi):
        f, g, new = fields[s], gs[s], fields[s + 1]

        def row(x):
            for y in range(YO, YO + ny, ROW):
                for h, c, total in around(g, i, x, y):
                    old = f[h, i, x, pl.ds(y, ROW), :]
                    new[h, i, x, pl.ds(y, ROW), :] = old + (time_step / H6) * (total - 6.0 * c)
        rows_of(XO + lo, XO + hi, GROUP, row)

    def pass_chem(i, lo, hi):
        def row(x):
            for y in range(YO, YO + ny, ROW):
                for h, c, total in around(w3, i, x, y):
                    chem[h, i, x - XO, pl.ds(y - YO, ROW), :] = (
                        (total - 6.0 * c) + bulk(f3, h, i, x, y))
        rows_of(XO + lo, XO + hi, GROUP, row)

    def relax(s, i, p):
        c = cut[s]
        pass_w(s, i, *span(p, -2, c - 1, nx + 2))
        pass_g(s, i, *span(p, -1, c - 2, nx + 1))
        pass_f(s, i, *span(p, 0, c - 3, nx))

    def potential(i, p):
        c = cut[RELAX]
        pass_w(RELAX, i, *span(p, -1, c - 1, nx + 1))
        pass_chem(i, *span(p, 0, c - 2, nx))

    def sums(lo, hi, acc):
        def body(x, acc):
            acc = list(acc)
            for y in range(0, ny, ROW):
                for h in range(2):
                    a = f3[h, 0, XO + x, pl.ds(YO + y, ROW), :]
                    b = f3[h, 1, XO + x, pl.ds(YO + y, ROW), :]
                    before = nb[h, 0, x, pl.ds(y, ROW), :]
                    after = nb[h, 1, x, pl.ds(y, ROW), :]
                    ca = chem[h, 0, x, pl.ds(y, ROW), :]
                    cb = chem[h, 1, x, pl.ds(y, ROW), :]
                    ta, tb = b - before, after - a
                    d, low, high = b - a, a - before, after - b
                    terms = (ta * ta, tb * tb, low * low, d * d, high * high, ca * ta, cb * tb)
                    acc = [u + v for u, v in zip(acc, terms)]
            return tuple(acc)
        return lax.fori_loop(lo, hi, body, acc)

    wait_load(0, cut[0], load_sem.at[0])
    split(0, cut[0])
    wait_load(cut[0], nx, load_sem.at[1])
    split(cut[0], nx)
    pl.semaphore_wait(barrier, len(partners))
    acc = tuple(jnp.zeros((ROW, LANES), jnp.float32) for _ in range(7))
    for word in ORDER:
        if word[0] == "t":
            p = int(word[1])
            for i in range(2):
                @pl.when(has[1 - i])
                def _():
                    chains[i, p].wait_recv()
            acc = sums(*span(p, 0, cut[RELAX] - 2, nx), acc)
            continue
        i, p = "abcd".index(word[1]) % 2, "abcd".index(word[1]) // 2
        if word[0] == "x":
            @pl.when(has[i])
            def _():
                chains[i, p].start()
            continue
        s = int(word[2])
        for c in halos[s, i, p]:
            if word[0] == "s":
                c.start()
            else:
                c.wait_recv()
        if word[0] == "r":
            relax(s, i, p)
        if word[0] == "p":
            potential(i, p)

    for n in range(7):
        mine[n : n + 1, :] = jnp.sum(acc[n], axis=0, keepdims=True)
    mine[7:8, :] = jnp.zeros((1, LANES), jnp.float32)
    group = 2 * gy_n
    me = gx * gy_n + gy
    copies = []
    for k in range(1, group):
        to = lax.rem(me + k, group)
        c = pltpu.make_async_remote_copy(
            src_ref=mine, dst_ref=rbuf.at[me], send_sem=red_send.at[k], recv_sem=red_recv.at[k],
            device_id={"gx": to // gy_n, "gy": lax.rem(to, gy_n)}, device_id_type=MESH)
        c.start()
        copies.append(c)
    rbuf[me] = mine[...]

    drops = [jnp.where(chain == end, 0.0, step_size / H6) for end in (0, chain_n - 1)]

    def prepare(x):
        for y in range(0, ny, ROW):
            at = pl.ds(y, ROW)
            f = [[f3[h, i, XO + x, pl.ds(YO + y, ROW), :] for h in range(2)] for i in range(2)]
            for i in range(2):
                rest = joined(*[f[i][h] * (1.0 / H2) - drops[i] * chem[h, i, x, at, :] for h in range(2)])
                if i == 0:
                    t = joined(*[jnp.where(has[0], f[1][h] - nb[h, 0, x, at, :], 0.0) for h in range(2)])
                else:
                    t = joined(*[jnp.where(has[1], nb[h, 1, x, at, :] - f[0][h], 0.0) for h in range(2)])
                for h in range(2):
                    chem[h, i, x, at, :] = rest[h]
                    tang[h, i, x, at, :] = t[h]
        for ref, dst in ((chem, rest_ref), (tang, tangent_ref)):
            for h in range(2):
                pltpu.make_async_copy(
                    ref.at[h, :, x, :, :],
                    dst.at[:, layer(x), :, pl.ds(h * LANES, LANES)], out_sem.at[0]).start()

    rows_of(0, nx, 2, prepare)
    for c in copies:
        c.wait_recv()
    total = rbuf[0]
    for k in range(1, group):
        total = total + rbuf[k]

    def mean(n, scaling):
        return jnp.sum(total[n : n + 1, :], axis=1, keepdims=True) * (1.0 / (cells * scaling))

    squares = [mean(n, H4) for n in range(5)]
    products = [mean(n, H6 * H2) for n in (5, 6)]

    def pull_of(tangent_sq, forward_sq, backward_sq, intersection, keep):
        scale = 1.0 / jnp.sqrt(tangent_sq + epsilon)
        along = intersection * scale
        spring = stiffness * (jnp.sqrt(forward_sq + epsilon) - jnp.sqrt(backward_sq + epsilon))
        pull = (step_size * along + spring) * scale * (1.0 / H2)
        return jnp.broadcast_to(jnp.where(keep, 0.0, pull), (1, pull_ref.shape[1]))

    pull_ref[0:1, :] = pull_of(squares[0], squares[3], squares[2], products[0], chain == 0)
    pull_ref[1:2, :] = pull_of(squares[1], squares[4], squares[3], products[1], chain == chain_n - 1)
    for ref in (chem, tang):
        pltpu.make_async_copy(ref, ref, out_sem.at[0]).wait()
    for c in [c for hs in halos.values() for c in hs] + copies:
        c.wait_send()
    for i in range(2):
        @pl.when(has[i])
        def _():
            for p in range(2):
                chains[i, p].wait_send()


def per_device(chain_n, gx_n, gy_n, v):
    _, nx, ny, nz = v.shape
    cells = nx * gx_n * ny * gy_n * nz

    def body(*refs):
        kernel(nx, ny, chain_n, gy_n, cells, *refs)

    padded = pltpu.VMEM((2, 2, nx + 2 * XO, ny + 2 * YO, LANES), jnp.float32)
    plain = pltpu.VMEM((2, 2, nx, ny, LANES), jnp.float32)
    dma = pltpu.SemaphoreType.DMA
    like = jax.ShapeDtypeStruct(v.shape, v.dtype)
    rest, tangent, pull = pl.pallas_call(
        body,
        out_shape=(like, like, jax.ShapeDtypeStruct((2, nz), jnp.float32)),
        in_specs=[pl.BlockSpec(memory_space=pltpu.HBM)],
        out_specs=(pl.BlockSpec(memory_space=pl.ANY), pl.BlockSpec(memory_space=pl.ANY),
                   pl.BlockSpec(memory_space=pltpu.VMEM)),
        scratch_shapes=[padded] * 11 + [
            plain, plain, plain,
            pltpu.VMEM((ROW, LANES), jnp.float32),
            pltpu.VMEM((2 * gy_n, ROW, LANES), jnp.float32),
            dma((2,)), dma((144,)), dma((144,)), dma((4,)), dma((4,)), dma((16,)), dma((16,)), dma((1,)),
        ],
        compiler_params=pltpu.CompilerParams(
            collective_id=0, has_side_effects=True, vmem_limit_bytes=42 * 1024 * 1024),
    )(v)
    return rest + pull[:, None, None, :] * tangent


def solution(mesh):
    sizes = [mesh.shape[a] for a in ("chain", "gx", "gy")]
    spec = P("chain", "gx", "gy", None)
    return jax.shard_map(
        lambda v: per_device(*sizes, v), mesh=mesh, in_specs=(spec,), out_specs=spec, check_vma=False)
```

```python
import jax
import jax.numpy as jnp
from jax import lax
from jax.experimental import pallas as pl
from jax.experimental.pallas import tpu as pltpu
from jax.sharding import PartitionSpec as P

RELAX = 3
spacing = 0.7853981633974483
undercool = -0.25
time_step = 0.00025
step_size = 0.002
stiffness = 0.5
epsilon = 1e-06

MESH = pl.DeviceIdType.MESH
LANES = 128
ROW = 8
XO = 3
YO = 8
H2 = spacing * spacing
H4 = H2 * H2
H6 = H4 * H2
GROUP = 8
MID = 22
ORDER = (
    "sa0", "lb", "sb0", "lc", "sc0", "ld", "ra0", "sa1", "rb0", "sb1", "sd0", "ra1", "sa2", "rb1",
    "sb2", "rc0", "sc1", "ra2", "xa", "rd0", "sd1", "rb2", "xb", "rc1", "sc2", "rd1", "sd2", "sa3",
    "rc2", "xc", "sb3", "rd2", "xd", "sc3", "sd3", "pa3", "pb3", "t0", "pc3", "pd3", "t1",
)


def around(ref, i, x, y):
    a = ref[0, i, x, pl.ds(y, ROW), :]
    b = ref[1, i, x, pl.ds(y, ROW), :]
    za = b + pltpu.roll(b, 1, 1)
    zb = a + pltpu.roll(a, LANES - 1, 1)
    out = []
    for h, c, z in ((0, a, za), (1, b, zb)):
        s = ref[h, i, x, pl.ds(y - 1, ROW), :] + ref[h, i, x, pl.ds(y + 1, ROW), :]
        s = s + (ref[h, i, x - 1, pl.ds(y, ROW), :] + ref[h, i, x + 1, pl.ds(y, ROW), :])
        out.append((h, c, s + z))
    return out


def rows_of(lo, hi, group, row):
    steps = (hi - lo) // group

    def body(n, _):
        for r in range(group):
            row(lo + n * group + r)
        return 0

    if steps:
        lax.fori_loop(0, steps, body, 0)
    for x in range(lo + steps * group, hi):
        row(x)


def kernel(nx, ny, chain_n, gy_n, cells, in_ref, rest_ref, tangent_ref, pull_ref,
           f0, f1, f2, f3, w0, w1, w2, w3, g0, g1, g2, chem, tang, nb, mine, rbuf,
           load_sem, halo_send, halo_recv, chain_send, chain_recv, red_send, red_recv, out_sem):
    fields, ws, gs = (f0, f1, f2, f3), (w0, w1, w2, w3), (g0, g1, g2)
    gx = lax.axis_index("gx")
    gy = lax.axis_index("gy")
    chain = lax.axis_index("chain")
    mate = 1 - gx
    up, down = lax.rem(gy + 1, gy_n), lax.rem(gy + gy_n - 1, gy_n)
    nxt, prv = lax.rem(chain + 1, chain_n), lax.rem(chain + chain_n - 1, chain_n)

    barrier = pltpu.get_barrier_semaphore()
    partners = (
        {"gx": mate}, {"gy": up}, {"gy": down}, {"gx": mate, "gy": up}, {"gx": mate, "gy": down},
        {"chain": nxt}, {"chain": prv},
    )
    for d in partners:
        pl.semaphore_signal(barrier, inc=1, device_id=d, device_id_type=MESH)

    cut = [MID * nx // 32 + 3 * (RELAX - s) for s in range(RELAX + 1)]

    def layer(x):
        return gx * (nx - 1) + (1 - 2 * gx) * x

    def start_load(lo, hi, sem):
        def body(x, _):
            for h in range(2):
                pltpu.make_async_copy(
                    in_ref.at[:, layer(x), :, pl.ds(h * LANES, LANES)],
                    chem.at[h, :, x, :, :], sem).start()
            return 0
        lax.fori_loop(lo, hi, body, 0)

    def wait_load(lo, hi, sem):
        view = chem.at[:, :, pl.ds(lo, hi - lo), :, :]
        pltpu.make_async_copy(view, view, sem).wait()

    lane = lax.broadcasted_iota(jnp.int32, (ROW, LANES), 1)
    half = LANES // 2
    low_half, even = lane < half, lane % 2 == 0
    twice = (2 * lane) % LANES
    halved = lane // 2

    def pick(v, index):
        return jnp.take_along_axis(v, index, axis=1)

    def split(i, lo, hi):
        def row(x):
            for y in range(0, ny, ROW):
                a = chem[0, i, x, pl.ds(y, ROW), :] * H2
                b = chem[1, i, x, pl.ds(y, ROW), :] * H2
                f0[0, i, XO + x, pl.ds(YO + y, ROW), :] = jnp.where(
                    low_half, pick(a, twice), pick(b, twice))
                f0[1, i, XO + x, pl.ds(YO + y, ROW), :] = jnp.where(
                    low_half, pick(a, twice + 1), pick(b, twice + 1))
        rows_of(lo, hi, 4, row)

    def joined(a, b):
        return (jnp.where(even, pick(a, halved), pick(b, halved)),
                jnp.where(even, pick(a, halved + half), pick(b, halved + half)))

    start_load(0, cut[0], load_sem.at[0])
    start_load(cut[0], nx, load_sem.at[1])

    def halo_copies(s, i, piece):
        f = fields[s]
        width = 3 if s < RELAX else 2
        lo, hi = span(piece, 0, cut[s], nx)
        rows = pl.ds(XO + lo, hi - lo)
        plan = [
            (f.at[:, i, rows, pl.ds(YO + ny - width, width), :],
             f.at[:, i, rows, pl.ds(YO - width, width), :], {"gy": up}),
            (f.at[:, i, rows, pl.ds(YO, width), :],
             f.at[:, i, rows, pl.ds(YO + ny, width), :], {"gy": down}),
        ]
        near = (lambda j: XO + j) if piece == 0 else (lambda j: XO + nx - 1 - j)
        far = (lambda j: XO - 1 - j) if piece == 0 else (lambda j: XO + nx + j)
        for j in range(width):
            plan.append((f.at[:, i, near(j), pl.ds(YO, ny), :],
                         f.at[:, i, far(j), pl.ds(YO, ny), :], {"gx": mate}))
        for j in range(width - 1):
            k = width - 1
            plan.append((f.at[:, i, near(j), pl.ds(YO + ny - k, k), :],
                         f.at[:, i, far(j), pl.ds(YO - k, k), :], {"gx": mate, "gy": up}))
            plan.append((f.at[:, i, near(j), pl.ds(YO, k), :],
                         f.at[:, i, far(j), pl.ds(YO + ny, k), :], {"gx": mate, "gy": down}))
        plan.sort(key=lambda copy: -len(copy[2]))
        base = ((2 * s + piece) * 2 + i) * 9
        return [
            pltpu.make_async_remote_copy(
                src_ref=src, dst_ref=dst, send_sem=halo_send.at[base + n],
                recv_sem=halo_recv.at[base + n], device_id=d, device_id_type=MESH)
            for n, (src, dst, d) in enumerate(plan)
        ]

    def span(p, start, mid, end):
        return (start, mid) if p == 0 else (mid, end)

    halos = {(s, i, p): halo_copies(s, i, p)
             for s in range(RELAX + 1) for i in range(2) for p in range(2)}

    has = (chain > 0, chain < chain_n - 1)

    def chain_copy(i, p):
        lo, hi = span(p, 0, cut[RELAX], nx)
        return pltpu.make_async_remote_copy(
            src_ref=f3.at[:, i, pl.ds(XO + lo, hi - lo), pl.ds(YO, ny), :],
            dst_ref=nb.at[:, 1 - i, pl.ds(lo, hi - lo), :, :],
            send_sem=chain_send.at[2 * p + i], recv_sem=chain_recv.at[2 * p + i],
            device_id={"chain": (prv, nxt)[i]}, device_id_type=MESH)

    chains = {(i, p): chain_copy(i, p) for i in range(2) for p in range(2)}

    def pass_w(s, i, lo, hi):
        f, w = fields[s], ws[s]

        def row(x):
            for y in range(YO - 2, YO + ny + 2, ROW):
                for h, c, total in around(f, i, x, y):
                    w[h, i, x, pl.ds(y, ROW), :] = total + (2.0 * H2 - 6.0) * c
        rows_of(XO + lo, XO + hi, GROUP, row)

    def bulk(f, h, i, x, y):
        c = f[h, i, x, pl.ds(y, ROW), :]
        return (c * c + (1.0 + undercool) * H4) * c

    def pass_g(s, i, lo, hi):
        f, w, g = fields[s], ws[s], gs[s]

        def row(x):
            for y in range(YO - 1, YO + ny + 1, ROW):
                for h, c, total in around(w, i, x, y):
                    g[h, i, x, pl.ds(y, ROW), :] = (total - 6.0 * c) + bulk(f, h, i, x, y)
        rows_of(XO + lo, XO + hi, GROUP, row)

    def pass_f(s, i, lo, hi):
        f, g, new = fields[s], gs[s], fields[s + 1]

        def row(x):
            for y in range(YO, YO + ny, ROW):
                for h, c, total in around(g, i, x, y):
                    old = f[h, i, x, pl.ds(y, ROW), :]
                    new[h, i, x, pl.ds(y, ROW), :] = old + (time_step / H6) * (total - 6.0 * c)
        rows_of(XO + lo, XO + hi, GROUP, row)

    def pass_chem(i, lo, hi):
        def row(x):
            for y in range(YO, YO + ny, ROW):
                for h, c, total in around(w3, i, x, y):
                    chem[h, i, x - XO, pl.ds(y - YO, ROW), :] = (
                        (total - 6.0 * c) + bulk(f3, h, i, x, y))
        rows_of(XO + lo, XO + hi, GROUP, row)

    def relax(s, i, p):
        c = cut[s]
        pass_w(s, i, *span(p, -2, c - 1, nx + 2))
        pass_g(s, i, *span(p, -1, c - 2, nx + 1))
        pass_f(s, i, *span(p, 0, c - 3, nx))

    def potential(i, p):
        c = cut[RELAX]
        pass_w(RELAX, i, *span(p, -1, c - 1, nx + 1))
        pass_chem(i, *span(p, 0, c - 2, nx))

    def sums(lo, hi, acc):
        def body(x, acc):
            acc = list(acc)
            for y in range(0, ny, ROW):
                for h in range(2):
                    a = f3[h, 0, XO + x, pl.ds(YO + y, ROW), :]
                    b = f3[h, 1, XO + x, pl.ds(YO + y, ROW), :]
                    before = nb[h, 0, x, pl.ds(y, ROW), :]
                    after = nb[h, 1, x, pl.ds(y, ROW), :]
                    ca = chem[h, 0, x, pl.ds(y, ROW), :]
                    cb = chem[h, 1, x, pl.ds(y, ROW), :]
                    ta, tb = b - before, after - a
                    d, low, high = b - a, a - before, after - b
                    terms = (ta * ta, tb * tb, low * low, d * d, high * high, ca * ta, cb * tb)
                    acc = [u + v for u, v in zip(acc, terms)]
            return tuple(acc)
        return lax.fori_loop(lo, hi, body, acc)

    wait_load(0, cut[0], load_sem.at[0])
    split(0, 0, cut[0])
    pl.semaphore_wait(barrier, len(partners))
    acc = tuple(jnp.zeros((ROW, LANES), jnp.float32) for _ in range(7))
    for word in ORDER:
        if word[0] == "t":
            p = int(word[1])
            for i in range(2):
                @pl.when(has[1 - i])
                def _():
                    chains[i, p].wait_recv()
            acc = sums(*span(p, 0, cut[RELAX] - 2, nx), acc)
            continue
        i, p = "abcd".index(word[1]) % 2, "abcd".index(word[1]) // 2
        if word == "lc":
            wait_load(cut[0], nx, load_sem.at[1])
        if word[0] == "l":
            split(i, *span(p, 0, cut[0], nx))
            continue
        if word[0] == "x":
            @pl.when(has[i])
            def _():
                chains[i, p].start()
            continue
        s = int(word[2])
        for c in halos[s, i, p]:
            if word[0] == "s":
                c.start()
            else:
                c.wait_recv()
        if word[0] == "r":
            relax(s, i, p)
        if word[0] == "p":
            potential(i, p)

    for n in range(7):
        mine[n : n + 1, :] = jnp.sum(acc[n], axis=0, keepdims=True)
    mine[7:8, :] = jnp.zeros((1, LANES), jnp.float32)
    group = 2 * gy_n
    me = gx * gy_n + gy
    copies = []
    for k in sorted(range(1, group), key=lambda k: -min(k % gy_n, gy_n - k % gy_n)):
        to = lax.rem(me + k, group)
        c = pltpu.make_async_remote_copy(
            src_ref=mine, dst_ref=rbuf.at[me], send_sem=red_send.at[k], recv_sem=red_recv.at[k],
            device_id={"gx": to // gy_n, "gy": lax.rem(to, gy_n)}, device_id_type=MESH)
        c.start()
        copies.append(c)
    rbuf[me] = mine[...]

    drops = [jnp.where(chain == end, 0.0, step_size / H6) for end in (0, chain_n - 1)]

    def prepare(x):
        for y in range(0, ny, ROW):
            at = pl.ds(y, ROW)
            f = [[f3[h, i, XO + x, pl.ds(YO + y, ROW), :] for h in range(2)] for i in range(2)]
            for i in range(2):
                rest = joined(*[f[i][h] * (1.0 / H2) - drops[i] * chem[h, i, x, at, :] for h in range(2)])
                if i == 0:
                    t = joined(*[jnp.where(has[0], f[1][h] - nb[h, 0, x, at, :], 0.0) for h in range(2)])
                else:
                    t = joined(*[jnp.where(has[1], nb[h, 1, x, at, :] - f[0][h], 0.0) for h in range(2)])
                for h in range(2):
                    chem[h, i, x, at, :] = rest[h]
                    tang[h, i, x, at, :] = t[h]
        for ref, dst in ((chem, rest_ref), (tang, tangent_ref)):
            for h in range(2):
                pltpu.make_async_copy(
                    ref.at[h, :, x, :, :],
                    dst.at[:, layer(x), :, pl.ds(h * LANES, LANES)], out_sem.at[0]).start()

    rows_of(0, nx, 2, prepare)
    for c in copies:
        c.wait_recv()
    total = rbuf[0]
    for k in range(1, group):
        total = total + rbuf[k]

    def mean(n, scaling):
        return jnp.sum(total[n : n + 1, :], axis=1, keepdims=True) * (1.0 / (cells * scaling))

    squares = [mean(n, H4) for n in range(5)]
    products = [mean(n, H6 * H2) for n in (5, 6)]

    def pull_of(tangent_sq, forward_sq, backward_sq, intersection, keep):
        scale = 1.0 / jnp.sqrt(tangent_sq + epsilon)
        along = intersection * scale
        spring = stiffness * (jnp.sqrt(forward_sq + epsilon) - jnp.sqrt(backward_sq + epsilon))
        pull = (step_size * along + spring) * scale * (1.0 / H2)
        return jnp.broadcast_to(jnp.where(keep, 0.0, pull), (1, pull_ref.shape[1]))

    pull_ref[0:1, :] = pull_of(squares[0], squares[3], squares[2], products[0], chain == 0)
    pull_ref[1:2, :] = pull_of(squares[1], squares[4], squares[3], products[1], chain == chain_n - 1)
    for ref in (chem, tang):
        pltpu.make_async_copy(ref, ref, out_sem.at[0]).wait()
    for c in [c for hs in halos.values() for c in hs] + copies:
        c.wait_send()
    for i in range(2):
        @pl.when(has[i])
        def _():
            for p in range(2):
                chains[i, p].wait_send()


def per_device(chain_n, gx_n, gy_n, v):
    _, nx, ny, nz = v.shape
    cells = nx * gx_n * ny * gy_n * nz

    def body(*refs):
        kernel(nx, ny, chain_n, gy_n, cells, *refs)

    padded = pltpu.VMEM((2, 2, nx + 2 * XO, ny + 2 * YO, LANES), jnp.float32)
    plain = pltpu.VMEM((2, 2, nx, ny, LANES), jnp.float32)
    dma = pltpu.SemaphoreType.DMA
    like = jax.ShapeDtypeStruct(v.shape, v.dtype)
    rest, tangent, pull = pl.pallas_call(
        body,
        out_shape=(like, like, jax.ShapeDtypeStruct((2, nz), jnp.float32)),
        in_specs=[pl.BlockSpec(memory_space=pltpu.HBM)],
        out_specs=(pl.BlockSpec(memory_space=pl.ANY), pl.BlockSpec(memory_space=pl.ANY),
                   pl.BlockSpec(memory_space=pltpu.VMEM)),
        scratch_shapes=[padded] * 11 + [
            plain, plain, plain,
            pltpu.VMEM((ROW, LANES), jnp.float32),
            pltpu.VMEM((2 * gy_n, ROW, LANES), jnp.float32),
            dma((2,)), dma((144,)), dma((144,)), dma((4,)), dma((4,)), dma((16,)), dma((16,)), dma((1,)),
        ],
        compiler_params=pltpu.CompilerParams(
            collective_id=0, has_side_effects=True, vmem_limit_bytes=50 * 1024 * 1024),
    )(v)
    return rest + pull[:, None, None, :] * tangent


def solution(mesh):
    sizes = [mesh.shape[a] for a in ("chain", "gx", "gy")]
    spec = P("chain", "gx", "gy", None)
    return jax.shard_map(
        lambda v: per_device(*sizes, v), mesh=mesh, in_specs=(spec,), out_specs=spec, check_vma=False)
```

```python
import jax
import jax.numpy as jnp
from jax import lax
from jax.experimental import pallas as pl
from jax.experimental.pallas import tpu as pltpu
from jax.sharding import PartitionSpec as P

RELAX = 3
spacing = 0.7853981633974483
undercool = -0.25
time_step = 0.00025
step_size = 0.002
stiffness = 0.5
epsilon = 1e-06

MESH = pl.DeviceIdType.MESH
LANES = 128
ROW = 8
XO = 3
YO = 8
H2 = spacing * spacing
H4 = H2 * H2
H6 = H4 * H2
GROUP = 8
MID = 22
ORDER = (
    "sa0", "lb", "sb0", "lc", "sc0", "ld", "ra0", "sa1", "rb0", "sb1", "sd0", "ra1", "sa2", "rb1",
    "sb2", "rc0", "sc1", "ra2", "xa", "rd0", "sd1", "rb2", "xb", "rc1", "sc2", "rd1", "sd2", "sa3",
    "rc2", "xc", "sb3", "rd2", "xd", "sc3", "sd3", "pa3", "pb3", "t0", "pc3", "pd3", "t1",
)


def around(ref, i, x, y):
    a = ref[0, i, x, pl.ds(y, ROW), :]
    b = ref[1, i, x, pl.ds(y, ROW), :]
    za = b + pltpu.roll(b, 1, 1)
    zb = a + pltpu.roll(a, LANES - 1, 1)
    out = []
    for h, c, z in ((0, a, za), (1, b, zb)):
        s = ref[h, i, x, pl.ds(y - 1, ROW), :] + ref[h, i, x, pl.ds(y + 1, ROW), :]
        s = s + (ref[h, i, x - 1, pl.ds(y, ROW), :] + ref[h, i, x + 1, pl.ds(y, ROW), :])
        out.append((h, c, s + z))
    return out


def rows_of(lo, hi, group, row):
    steps = (hi - lo) // group

    def body(n, _):
        for r in range(group):
            row(lo + n * group + r)
        return 0

    if steps:
        lax.fori_loop(0, steps, body, 0)
    for x in range(lo + steps * group, hi):
        row(x)


def kernel(nx, ny, chain_n, gy_n, cells, in_ref, rest_ref, tangent_ref, pull_ref,
           f0, f1, f2, f3, w0, w1, w2, w3, g0, g1, g2, chem, tang, nb, mine, rbuf,
           load_sem, halo_send, halo_recv, chain_send, chain_recv, red_send, red_recv, out_sem):
    fields, ws, gs = (f0, f1, f2, f3), (w0, w1, w2, w3), (g0, g1, g2)
    gx = lax.axis_index("gx")
    gy = lax.axis_index("gy")
    chain = lax.axis_index("chain")
    mate = 1 - gx
    up, down = lax.rem(gy + 1, gy_n), lax.rem(gy + gy_n - 1, gy_n)
    nxt, prv = lax.rem(chain + 1, chain_n), lax.rem(chain + chain_n - 1, chain_n)

    barrier = pltpu.get_barrier_semaphore()
    partners = (
        {"gx": mate}, {"gy": up}, {"gy": down}, {"gx": mate, "gy": up}, {"gx": mate, "gy": down},
        {"chain": nxt}, {"chain": prv},
    )
    for d in partners:
        pl.semaphore_signal(barrier, inc=1, device_id=d, device_id_type=MESH)

    cut = [MID * nx // 32 + 3 * (RELAX - s) for s in range(RELAX + 1)]

    def layer(x):
        return gx * (nx - 1) + (1 - 2 * gx) * x

    def start_load(lo, hi, sem):
        def body(x, _):
            for h in range(2):
                pltpu.make_async_copy(
                    in_ref.at[:, layer(x), :, pl.ds(h * LANES, LANES)],
                    chem.at[h, :, x, :, :], sem).start()
            return 0
        lax.fori_loop(lo, hi, body, 0)

    def wait_load(lo, hi, sem):
        view = chem.at[:, :, pl.ds(lo, hi - lo), :, :]
        pltpu.make_async_copy(view, view, sem).wait()

    lane = lax.broadcasted_iota(jnp.int32, (ROW, LANES), 1)
    half = LANES // 2
    low_half = lane < half
    apart = jnp.where(low_half, 2 * lane, 2 * lane - LANES + 1)
    together = lane // 2 + (lane % 2) * half

    def pick(v, index):
        return jnp.take_along_axis(v, index, axis=1)

    def swapped(a, b):
        return (jnp.where(low_half, a, pltpu.roll(b, half, 1)),
                jnp.where(low_half, pltpu.roll(a, half, 1), b))

    def split(i, lo, hi):
        def row(x):
            for y in range(0, ny, ROW):
                a = chem[0, i, x, pl.ds(y, ROW), :] * H2
                b = chem[1, i, x, pl.ds(y, ROW), :] * H2
                a, b = swapped(pick(a, apart), pick(b, apart))
                f0[0, i, XO + x, pl.ds(YO + y, ROW), :] = a
                f0[1, i, XO + x, pl.ds(YO + y, ROW), :] = b
        rows_of(lo, hi, 4, row)

    def joined(a, b):
        a, b = swapped(a, b)
        return pick(a, together), pick(b, together)

    start_load(0, cut[0], load_sem.at[0])
    start_load(cut[0], nx, load_sem.at[1])

    def halo_copies(s, i, piece):
        f = fields[s]
        width = 3 if s < RELAX else 2
        lo, hi = span(piece, 0, cut[s], nx)
        rows = pl.ds(XO + lo, hi - lo)
        plan = [
            (f.at[:, i, rows, pl.ds(YO + ny - width, width), :],
             f.at[:, i, rows, pl.ds(YO - width, width), :], {"gy": up}),
            (f.at[:, i, rows, pl.ds(YO, width), :],
             f.at[:, i, rows, pl.ds(YO + ny, width), :], {"gy": down}),
        ]
        near = (lambda j: XO + j) if piece == 0 else (lambda j: XO + nx - 1 - j)
        far = (lambda j: XO - 1 - j) if piece == 0 else (lambda j: XO + nx + j)
        for j in range(width):
            plan.append((f.at[:, i, near(j), pl.ds(YO, ny), :],
                         f.at[:, i, far(j), pl.ds(YO, ny), :], {"gx": mate}))
        for j in range(width - 1):
            k = width - 1
            plan.append((f.at[:, i, near(j), pl.ds(YO + ny - k, k), :],
                         f.at[:, i, far(j), pl.ds(YO - k, k), :], {"gx": mate, "gy": up}))
            plan.append((f.at[:, i, near(j), pl.ds(YO, k), :],
                         f.at[:, i, far(j), pl.ds(YO + ny, k), :], {"gx": mate, "gy": down}))
        plan.sort(key=lambda copy: -len(copy[2]))
        base = ((2 * s + piece) * 2 + i) * 9
        return [
            pltpu.make_async_remote_copy(
                src_ref=src, dst_ref=dst, send_sem=halo_send.at[base + n],
                recv_sem=halo_recv.at[base + n], device_id=d, device_id_type=MESH)
            for n, (src, dst, d) in enumerate(plan)
        ]

    def span(p, start, mid, end):
        return (start, mid) if p == 0 else (mid, end)

    halos = {(s, i, p): halo_copies(s, i, p)
             for s in range(RELAX + 1) for i in range(2) for p in range(2)}

    has = (chain > 0, chain < chain_n - 1)

    def chain_copy(i, p):
        lo, hi = span(p, 0, cut[RELAX], nx)
        return pltpu.make_async_remote_copy(
            src_ref=f3.at[:, i, pl.ds(XO + lo, hi - lo), pl.ds(YO, ny), :],
            dst_ref=nb.at[:, 1 - i, pl.ds(lo, hi - lo), :, :],
            send_sem=chain_send.at[2 * p + i], recv_sem=chain_recv.at[2 * p + i],
            device_id={"chain": (prv, nxt)[i]}, device_id_type=MESH)

    chains = {(i, p): chain_copy(i, p) for i in range(2) for p in range(2)}

    def pass_w(s, i, lo, hi):
        f, w = fields[s], ws[s]

        def row(x):
            for y in range(YO - 2, YO + ny + 2, ROW):
                for h, c, total in around(f, i, x, y):
                    w[h, i, x, pl.ds(y, ROW), :] = total + (2.0 * H2 - 6.0) * c
        rows_of(XO + lo, XO + hi, GROUP, row)

    def bulk(f, h, i, x, y):
        c = f[h, i, x, pl.ds(y, ROW), :]
        return (c * c + (1.0 + undercool) * H4) * c

    def pass_g(s, i, lo, hi):
        f, w, g = fields[s], ws[s], gs[s]

        def row(x):
            for y in range(YO - 1, YO + ny + 1, ROW):
                for h, c, total in around(w, i, x, y):
                    g[h, i, x, pl.ds(y, ROW), :] = (total - 6.0 * c) + bulk(f, h, i, x, y)
        rows_of(XO + lo, XO + hi, GROUP, row)

    def pass_f(s, i, lo, hi):
        f, g, new = fields[s], gs[s], fields[s + 1]

        def row(x):
            for y in range(YO, YO + ny, ROW):
                for h, c, total in around(g, i, x, y):
                    old = f[h, i, x, pl.ds(y, ROW), :]
                    new[h, i, x, pl.ds(y, ROW), :] = old + (time_step / H6) * (total - 6.0 * c)
        rows_of(XO + lo, XO + hi, GROUP, row)

    def pass_chem(i, lo, hi):
        def row(x):
            for y in range(YO, YO + ny, ROW):
                for h, c, total in around(w3, i, x, y):
                    chem[h, i, x - XO, pl.ds(y - YO, ROW), :] = (
                        (total - 6.0 * c) + bulk(f3, h, i, x, y))
        rows_of(XO + lo, XO + hi, GROUP, row)

    def relax(s, i, p):
        c = cut[s]
        pass_w(s, i, *span(p, -2, c - 1, nx + 2))
        pass_g(s, i, *span(p, -1, c - 2, nx + 1))
        pass_f(s, i, *span(p, 0, c - 3, nx))

    def potential(i, p):
        c = cut[RELAX]
        pass_w(RELAX, i, *span(p, -1, c - 1, nx + 1))
        pass_chem(i, *span(p, 0, c - 2, nx))

    def sums(lo, hi, acc):
        def body(x, acc):
            acc = list(acc)
            for y in range(0, ny, ROW):
                for h in range(2):
                    a = f3[h, 0, XO + x, pl.ds(YO + y, ROW), :]
                    b = f3[h, 1, XO + x, pl.ds(YO + y, ROW), :]
                    before = nb[h, 0, x, pl.ds(y, ROW), :]
                    after = nb[h, 1, x, pl.ds(y, ROW), :]
                    ca = chem[h, 0, x, pl.ds(y, ROW), :]
                    cb = chem[h, 1, x, pl.ds(y, ROW), :]
                    ta, tb = b - before, after - a
                    d, low, high = b - a, a - before, after - b
                    terms = (ta * ta, tb * tb, low * low, d * d, high * high, ca * ta, cb * tb)
                    acc = [u + v for u, v in zip(acc, terms)]
            return tuple(acc)
        return lax.fori_loop(lo, hi, body, acc)

    wait_load(0, cut[0], load_sem.at[0])
    split(0, 0, cut[0])
    pl.semaphore_wait(barrier, len(partners))
    acc = tuple(jnp.zeros((ROW, LANES), jnp.float32) for _ in range(7))
    for word in ORDER:
        if word[0] == "t":
            p = int(word[1])
            for i in range(2):
                @pl.when(has[1 - i])
                def _():
                    chains[i, p].wait_recv()
            acc = sums(*span(p, 0, cut[RELAX] - 2, nx), acc)
            continue
        i, p = "abcd".index(word[1]) % 2, "abcd".index(word[1]) // 2
        if word == "lc":
            wait_load(cut[0], nx, load_sem.at[1])
        if word[0] == "l":
            split(i, *span(p, 0, cut[0], nx))
            continue
        if word[0] == "x":
            @pl.when(has[i])
            def _():
                chains[i, p].start()
            continue
        s = int(word[2])
        for c in halos[s, i, p]:
            if word[0] == "s":
                c.start()
            else:
                c.wait_recv()
        if word[0] == "r":
            relax(s, i, p)
        if word[0] == "p":
            potential(i, p)

    for n in range(7):
        mine[n : n + 1, :] = jnp.sum(acc[n], axis=0, keepdims=True)
    mine[7:8, :] = jnp.zeros((1, LANES), jnp.float32)
    group = 2 * gy_n
    me = gx * gy_n + gy
    copies = []
    for k in sorted(range(1, group), key=lambda k: -min(k % gy_n, gy_n - k % gy_n)):
        to = lax.rem(me + k, group)
        c = pltpu.make_async_remote_copy(
            src_ref=mine, dst_ref=rbuf.at[me], send_sem=red_send.at[k], recv_sem=red_recv.at[k],
            device_id={"gx": to // gy_n, "gy": lax.rem(to, gy_n)}, device_id_type=MESH)
        c.start()
        copies.append(c)
    rbuf[me] = mine[...]

    drops = [jnp.where(chain == end, 0.0, step_size / H6) for end in (0, chain_n - 1)]

    def prepare(x):
        for y in range(0, ny, ROW):
            at = pl.ds(y, ROW)
            f = [[f3[h, i, XO + x, pl.ds(YO + y, ROW), :] for h in range(2)] for i in range(2)]
            for i in range(2):
                rest = joined(*[f[i][h] * (1.0 / H2) - drops[i] * chem[h, i, x, at, :] for h in range(2)])
                if i == 0:
                    t = joined(*[jnp.where(has[0], f[1][h] - nb[h, 0, x, at, :], 0.0) for h in range(2)])
                else:
                    t = joined(*[jnp.where(has[1], nb[h, 1, x, at, :] - f[0][h], 0.0) for h in range(2)])
                for h in range(2):
                    chem[h, i, x, at, :] = rest[h]
                    tang[h, i, x, at, :] = t[h]
        for ref, dst in ((chem, rest_ref), (tang, tangent_ref)):
            for h in range(2):
                pltpu.make_async_copy(
                    ref.at[h, :, x, :, :],
                    dst.at[:, layer(x), :, pl.ds(h * LANES, LANES)], out_sem.at[0]).start()

    rows_of(0, nx, 2, prepare)
    for c in copies:
        c.wait_recv()
    total = rbuf[0]
    for k in range(1, group):
        total = total + rbuf[k]

    def mean(n, scaling):
        return jnp.sum(total[n : n + 1, :], axis=1, keepdims=True) * (1.0 / (cells * scaling))

    squares = [mean(n, H4) for n in range(5)]
    products = [mean(n, H6 * H2) for n in (5, 6)]

    def pull_of(tangent_sq, forward_sq, backward_sq, intersection, keep):
        scale = 1.0 / jnp.sqrt(tangent_sq + epsilon)
        along = intersection * scale
        spring = stiffness * (jnp.sqrt(forward_sq + epsilon) - jnp.sqrt(backward_sq + epsilon))
        pull = (step_size * along + spring) * scale * (1.0 / H2)
        return jnp.broadcast_to(jnp.where(keep, 0.0, pull), (1, pull_ref.shape[1]))

    pull_ref[0:1, :] = pull_of(squares[0], squares[3], squares[2], products[0], chain == 0)
    pull_ref[1:2, :] = pull_of(squares[1], squares[4], squares[3], products[1], chain == chain_n - 1)
    for ref in (chem, tang):
        pltpu.make_async_copy(ref, ref, out_sem.at[0]).wait()
    for c in [c for hs in halos.values() for c in hs] + copies:
        c.wait_send()
    for i in range(2):
        @pl.when(has[i])
        def _():
            for p in range(2):
                chains[i, p].wait_send()


def per_device(chain_n, gx_n, gy_n, v):
    _, nx, ny, nz = v.shape
    cells = nx * gx_n * ny * gy_n * nz

    def body(*refs):
        kernel(nx, ny, chain_n, gy_n, cells, *refs)

    padded = pltpu.VMEM((2, 2, nx + 2 * XO, ny + 2 * YO, LANES), jnp.float32)
    plain = pltpu.VMEM((2, 2, nx, ny, LANES), jnp.float32)
    dma = pltpu.SemaphoreType.DMA
    like = jax.ShapeDtypeStruct(v.shape, v.dtype)
    rest, tangent, pull = pl.pallas_call(
        body,
        out_shape=(like, like, jax.ShapeDtypeStruct((2, nz), jnp.float32)),
        in_specs=[pl.BlockSpec(memory_space=pltpu.HBM)],
        out_specs=(pl.BlockSpec(memory_space=pl.ANY), pl.BlockSpec(memory_space=pl.ANY),
                   pl.BlockSpec(memory_space=pltpu.VMEM)),
        scratch_shapes=[padded] * 11 + [
            plain, plain, plain,
            pltpu.VMEM((ROW, LANES), jnp.float32),
            pltpu.VMEM((2 * gy_n, ROW, LANES), jnp.float32),
            dma((2,)), dma((144,)), dma((144,)), dma((4,)), dma((4,)), dma((16,)), dma((16,)), dma((1,)),
        ],
        compiler_params=pltpu.CompilerParams(
            collective_id=0, has_side_effects=True, vmem_limit_bytes=50 * 1024 * 1024),
    )(v)
    return rest + pull[:, None, None, :] * tangent


def solution(mesh):
    sizes = [mesh.shape[a] for a in ("chain", "gx", "gy")]
    spec = P("chain", "gx", "gy", None)
    return jax.shard_map(
        lambda v: per_device(*sizes, v), mesh=mesh, in_specs=(spec,), out_specs=spec, check_vma=False)
```
